512 devices in a mesh: wide: 64 (over y, z), narrow: 8 (over x, core).
Axes of the slice: x: 4, y: 8, z: 8, core: 2. Of those that a mesh axis runs over, the one named last changes fastest.
Arguments:
- node_rows: bfloat16 [1048576, 128], P(('wide', 'narrow')), may hold values from -6 to 6
- tile_values: bfloat16 [8192, 128, 128], P(('wide', 'narrow')), may hold values from -0.25 to 0.25
- tile_owner: int32 [8192, 1], P(('wide', 'narrow')), may hold values from 0 to 63; in each aligned block of 16 rows (0 to 15, 16 to 31, ...) at most 2 rows name the same one
- tile_block: int32 [8192], P(('wide', 'narrow')), may hold values from 0 to 15
- edge_degree: int32 [65536], P('wide'), may hold values from 1 to 4
- w_in: bfloat16 [128, 512], replicated, may hold values from -0.5 to 0.5
- w_out: bfloat16 [512, 128], replicated, may hold values from -0.25 to 0.25
Outputs:
- node_out: bfloat16 [1048576, 128], P(('wide', 'narrow'))
The draws below stay inside these ranges and needn't reach their ends.
Inputs may be any that keep to these rules, and one draw needn't show every extreme that they name: `tile_owner`: among the 16 tiles of one device at most 2 name the same owner, and in every draw some device has 2 tiles that name one owner.
All inputs are finite; a program needn't handle non-finite values.
Results may differ from the reference program's by a relative error of at most 0.0038.
Values may be sent and summed in bfloat16 or wider, within the bound.
A program may use at most 192 MiB of HBM per device.

```python
import math
import jax
import jax.numpy as jnp
import numpy as np
from jax import lax

B = 128
C = 128
HID = 512
K = 2
ROUNDS = 1
NB_DEV = 16
EB_W = 8
OWNERS = 64
STRIPS = 8
TILES_DEV = 16
CAP = 2
NODES = 1048576
EDGES = 65536
TILES = 8192


def plant(entries, rng, smallest, largest):
    place = [jax.random.randint(jax.random.fold_in(rng, axis), (), 0, length) for axis, length in enumerate(entries.shape)]
    main_axis = entries.shape.index(max(entries.shape))
    next_to = place[:main_axis] + [(place[main_axis] + 1) % entries.shape[main_axis]] + place[main_axis + 1:]
    return entries.at[tuple(place)].set(smallest).at[tuple(next_to)].set(largest)


def shard_levels(key, extent, split, low, largest):
    loudness = 1.0
    for dim, blocks in split:
        draws = jax.random.uniform(jax.random.fold_in(jax.random.fold_in(key, 6), dim), (blocks,), jnp.float32, low / len(split), largest / len(split))
        loudness = loudness * jnp.repeat(jnp.exp(draws), extent[dim] // blocks).reshape((-1,) + (1,) * (len(extent) - 1 - dim))
    return loudness


def shared_out(key, own, number, rows, number_of, top, limit, slope):
    order = jax.random.permutation(key, number_of)
    heavy_load, ordinary = portions_of(number_of, rows * top, limit, slope, True), portions_of(number_of, rows * top, limit, slope, False)
    places = jnp.arange(number_of)

    def named(tallies, offset_by):
        used = int((tallies > 0).sum())
        fixed = max(1, used // 4)
        passed = fixed + (places - fixed + offset_by * (used - fixed)) % max(1, number_of - fixed)
        return jnp.zeros((number_of,), jnp.int32).at[order[jnp.where(places < fixed, places, passed)]].set(jnp.asarray(tallies, jnp.int32))

    tallies = jnp.where(number % 4 == 0, named(heavy_load, number // 4), named(ordinary, number - number // 4 - 1))
    mixed = jax.random.permutation(jax.random.fold_in(own, 3), number_of)
    giver, receiver = mixed[0:number_of // 2 * 2:2], mixed[1:number_of // 2 * 2:2]
    room = jnp.minimum(tallies[giver] - 1, limit - tallies[receiver]) // 2
    room = jnp.where((giver == order[0]) | (receiver == order[0]) | (tallies[receiver] == 0), 0, jnp.maximum(room, 0))
    passed = jax.random.randint(jax.random.fold_in(own, 4), (number_of // 2,), 0, 1 << 20) % (room + 1)
    tallies = tallies.at[giver].add(-passed).at[receiver].add(passed)
    members = jnp.searchsorted(jnp.cumsum(tallies), jnp.arange(rows * top), side="right").astype(jnp.int32)
    listing = members.reshape(top, rows).T
    listing = listing[jax.random.permutation(jax.random.fold_in(own, 1), rows)]
    offset_by = jax.random.randint(jax.random.fold_in(own, 2), (rows, 1), 0, top)
    return jnp.take_along_axis(listing, (jnp.arange(top)[None, :] + offset_by) % top, axis=1)


def portions_of(count, total, bound, skew, full):
    loads = [(1 << 20) // math.isqrt(grade ** skew) + 1 for grade in range(1, count + 1)]
    largest = bound if full else min(bound, max(-(-total // count), total * loads[0] // sum(loads)))
    least = 1 if total - largest >= count - 1 else 0
    holding, spare = [largest] + [least] * (count - 1), total - largest - least * (count - 1)
    while spare > 0:
        movable = [i for i in range(1, count) if holding[i] < largest] or [i for i in range(1, count) if holding[i] < bound]
        mass, budget = sum([loads[i] for i in movable]), spare
        for i in movable:
            addition = min(bound - holding[i], max(1, budget * loads[i] // mass), spare)
            holding[i] = holding[i] + addition
            spare = spare - addition
    return np.array(holding)


def normal_values(key, shape, scale, reach, split=(), kind=jnp.bfloat16):
    entries = scale * jax.random.normal(key, shape, jnp.float32)
    if split:
        entries = entries * shard_levels(key, shape, split, -0.22, 0.18)
    return jnp.clip(entries, -reach, reach).astype(kind)


def setup_inputs(seed: int = 0) -> dict:
    seeds = jax.random.split(jax.random.key(seed), 8)
    node_rows = normal_values(seeds[0], (NODES, C), 1.0, 6.0, ((0, 512),))
    tile_values = normal_values(seeds[1], (TILES, B, B), (B * K * STRIPS // 4) ** -0.5, 0.25, ((0, 512),))
    tile_owner_keys = jax.random.split(jax.random.fold_in(seeds[2], 1), TILES // TILES_DEV)
    tile_owner_turns = jax.random.permutation(jax.random.fold_in(seeds[2], 3), TILES // TILES_DEV)
    tile_owner = jax.vmap(lambda own, number: shared_out(jax.random.fold_in(seeds[2], 2), own, number, TILES_DEV, OWNERS, 1, CAP, 2))(tile_owner_keys, tile_owner_turns).reshape((TILES, 1))
    tile_block = plant(jax.random.randint(seeds[3], (TILES,), 0, NB_DEV), jax.random.fold_in(seeds[3], 1), 0, NB_DEV - 1).astype(jnp.int32)
    edge_degree = plant(jax.random.randint(seeds[4], (EDGES,), 1, 5), jax.random.fold_in(seeds[4], 1), 1, 4).astype(jnp.int32)
    w_in = normal_values(seeds[5], (C, HID), C ** -0.5, 0.5)
    w_out = normal_values(seeds[6], (HID, C), HID ** -0.5, 0.25)
    return {"node_rows": node_rows, "tile_values": tile_values, "tile_owner": tile_owner, "tile_block": tile_block, "edge_degree": edge_degree, "w_in": w_in, "w_out": w_out}


def edge_phase(node_blocks, tiles_w, owner_w, block_w, degree_w, w_in, w_out):
    strip_ids = jnp.arange(STRIPS, dtype=jnp.int32)[:, None]
    global_block = ((owner_w * STRIPS + strip_ids) * NB_DEV + block_w).astype(jnp.int32)
    node_pick = node_blocks[global_block]
    products = jnp.einsum("rtij,rtjc->rtic", tiles_w.astype(jnp.float32), node_pick.astype(jnp.float32))
    edge_sum = jnp.sum(products.reshape(STRIPS, EB_W, K, B, C), axis=(0, 2)).reshape(EB_W * B, C)
    edge_in = (edge_sum / degree_w.astype(jnp.float32)[:, None]).astype(jnp.bfloat16)
    pre_act = jnp.dot(edge_in, w_in, preferred_element_type=jnp.float32)
    hidden = jax.nn.silu(pre_act).astype(jnp.bfloat16)
    edge_out = jnp.dot(hidden, w_out, preferred_element_type=jnp.float32).astype(jnp.bfloat16)
    blocks_out = edge_out.reshape(EB_W, B, C).astype(jnp.float32)
    grouped = tiles_w.reshape(STRIPS, EB_W, K, B, B).astype(jnp.float32)
    tile_terms = jnp.einsum("rekji,ejc->rekic", grouped, blocks_out).astype(jnp.bfloat16)
    return global_block.reshape(STRIPS * TILES_DEV), tile_terms.reshape(STRIPS * TILES_DEV, B, C)


def reference(node_rows, tile_values, tile_owner, tile_block, edge_degree, w_in, w_out):
    tiles = tile_values.reshape(OWNERS, STRIPS, TILES_DEV, B, B)
    owners = tile_owner.reshape(OWNERS, STRIPS, TILES_DEV)
    blocks = tile_block.reshape(OWNERS, STRIPS, TILES_DEV)
    degrees = edge_degree.reshape(OWNERS, EB_W * B)
    current = node_rows
    for round_index in range(ROUNDS):
        node_blocks = current.reshape(NODES // B, B, C)

        def visit_owner(node_total, inputs):
            tiles_w, owner_w, block_w, degree_w = inputs
            global_block, tile_terms = edge_phase(node_blocks, tiles_w, owner_w, block_w, degree_w, w_in, w_out)
            node_total = node_total.at[global_block].add(tile_terms.astype(jnp.float32))
            return node_total, None

        start_total = jnp.zeros((NODES // B, B, C), jnp.float32)
        node_total, _ = lax.scan(visit_owner, start_total, (tiles, owners, blocks, degrees))
        current = (current.astype(jnp.float32) + node_total.reshape(NODES, C)).astype(jnp.bfloat16)
    return current
```

```python
import jax
import jax.numpy as jnp
from jax import lax
from jax.sharding import PartitionSpec as P


def edge_network(summed, degrees, w_in, w_out):
    edge_in = (summed / degrees.astype(jnp.float32)[:, None]).astype(jnp.bfloat16)
    pre_act = jnp.dot(edge_in, w_in, preferred_element_type=jnp.float32)
    hidden = jax.nn.silu(pre_act).astype(jnp.bfloat16)
    return jnp.dot(hidden, w_out, preferred_element_type=jnp.float32).astype(jnp.bfloat16)


def body(node_rows, tile_values, tile_owner, tile_block, edge_degree, w_in, w_out):
    owners = lax.axis_size("wide")
    tile_count, block_size, _ = tile_values.shape
    channels = node_rows.shape[1]
    node_block_count = node_rows.shape[0] // block_size
    edge_row_count = edge_degree.shape[0]
    edge_blocks = edge_row_count // block_size
    per_block = tile_count // edge_blocks
    capacity = max(2, 2 * tile_count // owners)
    slot_count = owners * capacity
    target = tile_owner[:, 0]
    positions = jnp.arange(tile_count, dtype=jnp.int32)
    earlier = (target[:, None] == target[None, :]) & (positions[None, :] < positions[:, None])
    order_in = jnp.sum(earlier.astype(jnp.int32), axis=1)
    slot_of = target * capacity + order_in
    slot_ids = jnp.arange(slot_count, dtype=jnp.int32)
    matches = slot_of[:, None] == slot_ids[None, :]
    wanted_out = jnp.sum(jnp.where(matches, tile_block[:, None] + 1, 0), axis=0) - 1
    wanted = lax.all_to_all(
        wanted_out.reshape(owners, capacity), "wide", split_axis=0, concat_axis=0, tiled=True
    ).reshape(slot_count)
    filled = wanted >= 0
    block_ids = jnp.arange(node_block_count, dtype=jnp.int32)
    selector = (wanted[None, :] == block_ids[:, None]).astype(jnp.bfloat16)
    grouped = tile_values.reshape(edge_blocks, per_block, block_size, block_size)
    current = node_rows
    node_blocks = current.reshape(node_block_count, block_size, channels)
    picked = jnp.where(
        filled[:, None, None], node_blocks[jnp.maximum(wanted, 0)], jnp.zeros((), jnp.bfloat16)
    )
    arrived = lax.all_to_all(
        picked.reshape(owners, capacity, block_size, channels),
        "wide",
        split_axis=0,
        concat_axis=0,
        tiled=True,
    )
    tile_rows = arrived.reshape(slot_count, block_size, channels)[slot_of]
    partial_value = jnp.einsum(
        "tij,tjc->tic", tile_values, tile_rows, preferred_element_type=jnp.float32
    )
    partial_value = jnp.sum(
        partial_value.reshape(edge_blocks, per_block, block_size, channels), axis=1
    )
    groups = lax.axis_size("narrow")
    me = lax.axis_index("narrow")
    own_rows = edge_row_count // groups
    pieces = lax.all_to_all(
        partial_value.reshape(groups, own_rows, channels), "narrow", 0, 0, tiled=True
    )
    summed = jnp.sum(pieces, axis=0)
    own_degree = lax.dynamic_slice_in_dim(edge_degree, me * own_rows, own_rows)
    own_out = edge_network(summed, own_degree, w_in, w_out)
    edge_out = lax.all_to_all(
        jnp.broadcast_to(own_out[None], (groups, own_rows, channels)), "narrow", 0, 0, tiled=True
    )
    blocks_out = edge_out.reshape(edge_blocks, block_size, channels)
    tile_terms = jnp.einsum(
        "ekji,ejc->ekic", grouped, blocks_out, preferred_element_type=jnp.float32
    ).astype(jnp.bfloat16)
    outgoing = jnp.zeros((slot_count, block_size, channels), jnp.bfloat16)
    outgoing = outgoing.at[slot_of].set(tile_terms.reshape(tile_count, block_size, channels))
    returned = lax.all_to_all(
        outgoing.reshape(owners, capacity, block_size, channels),
        "wide",
        split_axis=0,
        concat_axis=0,
        tiled=True,
    )
    gathered = jnp.dot(
        selector,
        returned.reshape(slot_count, block_size * channels),
        preferred_element_type=jnp.float32,
    )
    current = (
        current.astype(jnp.float32) + gathered.reshape(node_block_count * block_size, channels)
    ).astype(jnp.bfloat16)
    return current


def solution(mesh):
    return jax.shard_map(
        body,
        mesh=mesh,
        in_specs=(
            P(("wide", "narrow"), None),
            P(("wide", "narrow"), None, None),
            P(("wide", "narrow"), None),
            P(("wide", "narrow")),
            P("wide"),
            P(),
            P(),
        ),
        out_specs=P(("wide", "narrow"), None),
        check_vma=False,
    )
```

```python
import jax
import jax.numpy as jnp
from jax import lax
from jax.sharding import PartitionSpec as P


def edge_network(summed, degrees, w_in, w_out):
    edge_in = (summed / degrees.astype(jnp.float32)[:, None]).astype(jnp.bfloat16)
    pre_act = jnp.dot(edge_in, w_in, preferred_element_type=jnp.float32)
    hidden = jax.nn.silu(pre_act).astype(jnp.bfloat16)
    return jnp.dot(hidden, w_out, preferred_element_type=jnp.float32).astype(jnp.bfloat16)


def body(node_rows, tile_values, tile_owner, tile_block, edge_degree, w_in, w_out):
    owners = lax.axis_size("wide")
    tile_count, block_size, _ = tile_values.shape
    channels = node_rows.shape[1]
    node_block_count = node_rows.shape[0] // block_size
    edge_row_count = edge_degree.shape[0]
    edge_blocks = edge_row_count // block_size
    per_block = tile_count // edge_blocks
    capacity = max(2, 2 * tile_count // owners)
    slot_count = owners * capacity
    target = tile_owner[:, 0]
    positions = jnp.arange(tile_count, dtype=jnp.int32)
    earlier = (target[:, None] == target[None, :]) & (positions[None, :] < positions[:, None])
    order_in = jnp.sum(earlier.astype(jnp.int32), axis=1)
    slot_of = target * capacity + order_in
    slot_ids = jnp.arange(slot_count, dtype=jnp.int32)
    matches = slot_of[:, None] == slot_ids[None, :]
    wanted_out = jnp.sum(jnp.where(matches, tile_block[:, None] + 1, 0), axis=0) - 1
    wanted = lax.all_to_all(
        wanted_out.reshape(owners, capacity), "wide", split_axis=0, concat_axis=0, tiled=True
    ).reshape(slot_count)
    block_ids = jnp.arange(node_block_count, dtype=jnp.int32)
    selector = (wanted[None, :] == block_ids[:, None]).astype(jnp.bfloat16)
    grouped = tile_values.reshape(edge_blocks, per_block, block_size, block_size)
    current = node_rows
    node_blocks = current.reshape(node_block_count, block_size, channels)
    picked = node_blocks[jnp.maximum(wanted, 0)]
    arrived = lax.all_to_all(
        picked.reshape(owners, capacity, block_size, channels),
        "wide",
        split_axis=0,
        concat_axis=0,
        tiled=True,
    )
    tile_rows = arrived.reshape(slot_count, block_size, channels)[slot_of]
    partial_value = jnp.einsum(
        "tij,tjc->tic", tile_values, tile_rows, preferred_element_type=jnp.float32
    )
    partial_value = jnp.sum(
        partial_value.reshape(edge_blocks, per_block, block_size, channels), axis=1
    )
    groups = lax.axis_size("narrow")
    me = lax.axis_index("narrow")
    own_rows = edge_row_count // groups
    pieces = lax.all_to_all(
        partial_value.reshape(groups, own_rows, channels), "narrow", 0, 0, tiled=True
    )
    summed = jnp.sum(pieces, axis=0)
    own_degree = lax.dynamic_slice_in_dim(edge_degree, me * own_rows, own_rows)
    own_out = edge_network(summed, own_degree, w_in, w_out)
    edge_out = lax.all_to_all(
        jnp.broadcast_to(own_out[None], (groups, own_rows, channels)), "narrow", 0, 0, tiled=True
    )
    blocks_out = edge_out.reshape(edge_blocks, block_size, channels)
    tile_terms = jnp.einsum(
        "ekji,ejc->ekic", grouped, blocks_out, preferred_element_type=jnp.float32
    ).astype(jnp.bfloat16)
    tile_of_slot = jnp.sum(jnp.where(matches, positions[:, None], 0), axis=0)
    outgoing = tile_terms.reshape(tile_count, block_size, channels)[tile_of_slot]
    returned = lax.all_to_all(
        outgoing.reshape(owners, capacity, block_size, channels),
        "wide",
        split_axis=0,
        concat_axis=0,
        tiled=True,
    )
    gathered = jnp.dot(
        selector,
        returned.reshape(slot_count, block_size * channels),
        preferred_element_type=jnp.float32,
    )
    current = (
        current.astype(jnp.float32) + gathered.reshape(node_block_count * block_size, channels)
    ).astype(jnp.bfloat16)
    return current


def solution(mesh):
    return jax.shard_map(
        body,
        mesh=mesh,
        in_specs=(
            P(("wide", "narrow"), None),
            P(("wide", "narrow"), None, None),
            P(("wide", "narrow"), None),
            P(("wide", "narrow")),
            P("wide"),
            P(),
            P(),
        ),
        out_specs=P(("wide", "narrow"), None),
        check_vma=False,
    )
```

```python
import functools

import jax
import jax.numpy as jnp
from jax import lax
from jax.experimental import pallas as pl
from jax.experimental.pallas import tpu as pltpu
from jax.sharding import PartitionSpec as P
MESH = pl.DeviceIdType.MESH


def _edge_kernel(groups, parts_ref, degree_ref, w_in_ref, w_out_ref, out_ref,
                 inbox, stage, send_a, recv_a, send_b, recv_b):
    me = lax.axis_index("narrow")
    col = lax.axis_index("wide")
    barrier = pltpu.get_barrier_semaphore()
    for k in range(1, groups):
        pl.semaphore_signal(barrier, inc=1, device_id=(col, lax.rem(me + k, groups)), device_id_type=MESH)
    pl.semaphore_wait(barrier, groups - 1)

    def first(d):
        return pltpu.make_async_remote_copy(
            src_ref=parts_ref.at[d], dst_ref=inbox.at[me], send_sem=send_a.at[d],
            recv_sem=recv_a.at[me], device_id=(col, d), device_id_type=MESH)

    for k in range(1, groups):
        first(lax.rem(me + k, groups)).start()
    total = parts_ref[me]
    for k in range(1, groups):
        d = lax.rem(me + k, groups)
        s = lax.rem(me + groups - k, groups)
        first(d).wait_send()
        pltpu.make_async_remote_copy(
            src_ref=parts_ref.at[s], dst_ref=inbox.at[s], send_sem=send_a.at[s],
            recv_sem=recv_a.at[s], device_id=(col, s), device_id_type=MESH).wait_recv()
        total = total + inbox[s]
    edge_in = (total / degree_ref[...]).astype(jnp.bfloat16)
    pre = jnp.dot(edge_in, w_in_ref[...], preferred_element_type=jnp.float32)
    hidden = (pre * jax.nn.sigmoid(pre)).astype(jnp.bfloat16)
    own = jnp.dot(hidden, w_out_ref[...], preferred_element_type=jnp.float32).astype(jnp.bfloat16)
    stage[...] = own
    out_ref[me] = own

    def second(d):
        return pltpu.make_async_remote_copy(
            src_ref=stage, dst_ref=out_ref.at[me], send_sem=send_b.at[d],
            recv_sem=recv_b.at[me], device_id=(col, d), device_id_type=MESH)

    for k in range(1, groups):
        second(lax.rem(me + k, groups)).start()
    for k in range(1, groups):
        d = lax.rem(me + k, groups)
        s = lax.rem(me + groups - k, groups)
        second(d).wait_send()
        pltpu.make_async_remote_copy(
            src_ref=stage, dst_ref=out_ref.at[s], send_sem=send_b.at[s],
            recv_sem=recv_b.at[s], device_id=(col, s), device_id_type=MESH).wait_recv()


def edge_exchange(parts, degree, w_in, w_out, collective_id):
    groups, rows, channels = parts.shape
    vmem = pl.BlockSpec(memory_space=pltpu.VMEM)
    return pl.pallas_call(
        functools.partial(_edge_kernel, groups),
        out_shape=jax.ShapeDtypeStruct((groups, rows, channels), jnp.bfloat16),
        in_specs=[vmem] * 4,
        out_specs=vmem,
        scratch_shapes=[
            pltpu.VMEM((groups, rows, channels), jnp.float32),
            pltpu.VMEM((rows, channels), jnp.bfloat16),
            pltpu.SemaphoreType.DMA((groups,)), pltpu.SemaphoreType.DMA((groups,)),
            pltpu.SemaphoreType.DMA((groups,)), pltpu.SemaphoreType.DMA((groups,)),
        ],
        compiler_params=pltpu.CompilerParams(collective_id=collective_id, has_side_effects=True),
    )(parts, degree, w_in, w_out)


def edge_network(summed, degrees, w_in, w_out):
    edge_in = (summed / degrees.astype(jnp.float32)[:, None]).astype(jnp.bfloat16)
    pre_act = jnp.dot(edge_in, w_in, preferred_element_type=jnp.float32)
    hidden = jax.nn.silu(pre_act).astype(jnp.bfloat16)
    return jnp.dot(hidden, w_out, preferred_element_type=jnp.float32).astype(jnp.bfloat16)


def body(node_rows, tile_values, tile_owner, tile_block, edge_degree, w_in, w_out):
    owners = lax.axis_size("wide")
    tile_count, block_size, _ = tile_values.shape
    channels = node_rows.shape[1]
    node_block_count = node_rows.shape[0] // block_size
    edge_row_count = edge_degree.shape[0]
    edge_blocks = edge_row_count // block_size
    per_block = tile_count // edge_blocks
    capacity = max(2, 2 * tile_count // owners)
    slot_count = owners * capacity
    target = tile_owner[:, 0]
    positions = jnp.arange(tile_count, dtype=jnp.int32)
    earlier = (target[:, None] == target[None, :]) & (positions[None, :] < positions[:, None])
    order_in = jnp.sum(earlier.astype(jnp.int32), axis=1)
    slot_of = target * capacity + order_in
    slot_ids = jnp.arange(slot_count, dtype=jnp.int32)
    matches = slot_of[:, None] == slot_ids[None, :]
    wanted_out = jnp.sum(jnp.where(matches, tile_block[:, None] + 1, 0), axis=0) - 1
    wanted = lax.all_to_all(
        wanted_out.reshape(owners, capacity), "wide", split_axis=0, concat_axis=0, tiled=True
    ).reshape(slot_count)
    block_ids = jnp.arange(node_block_count, dtype=jnp.int32)
    selector = (wanted[None, :] == block_ids[:, None]).astype(jnp.bfloat16)
    grouped = tile_values.reshape(edge_blocks, per_block, block_size, block_size)
    current = node_rows
    node_blocks = current.reshape(node_block_count, block_size, channels)
    picked = node_blocks[jnp.maximum(wanted, 0)]
    arrived = lax.all_to_all(
        picked.reshape(owners, capacity, block_size, channels),
        "wide",
        split_axis=0,
        concat_axis=0,
        tiled=True,
    )
    tile_rows = arrived.reshape(slot_count, block_size, channels)[slot_of]
    partial_value = jnp.einsum(
        "tij,tjc->tic", tile_values, tile_rows, preferred_element_type=jnp.float32
    )
    partial_value = jnp.sum(
        partial_value.reshape(edge_blocks, per_block, block_size, channels), axis=1
    )
    groups = lax.axis_size("narrow")
    me = lax.axis_index("narrow")
    own_rows = edge_row_count // groups
    own_degree = lax.dynamic_slice_in_dim(edge_degree, me * own_rows, own_rows)
    edge_out = edge_exchange(
        partial_value.reshape(groups, own_rows, channels),
        own_degree.astype(jnp.float32)[:, None],
        w_in,
        w_out,
        0,
    )
    blocks_out = edge_out.reshape(edge_blocks, block_size, channels)
    tile_terms = jnp.einsum(
        "ekji,ejc->ekic", grouped, blocks_out, preferred_element_type=jnp.float32
    ).astype(jnp.bfloat16)
    tile_of_slot = jnp.sum(jnp.where(matches, positions[:, None], 0), axis=0)
    outgoing = tile_terms.reshape(tile_count, block_size, channels)[tile_of_slot]
    returned = lax.all_to_all(
        outgoing.reshape(owners, capacity, block_size, channels),
        "wide",
        split_axis=0,
        concat_axis=0,
        tiled=True,
    )
    gathered = jnp.dot(
        selector,
        returned.reshape(slot_count, block_size * channels),
        preferred_element_type=jnp.float32,
    )
    current = (
        current.astype(jnp.float32) + gathered.reshape(node_block_count * block_size, channels)
    ).astype(jnp.bfloat16)
    return current


def solution(mesh):
    return jax.shard_map(
        body,
        mesh=mesh,
        in_specs=(
            P(("wide", "narrow"), None),
            P(("wide", "narrow"), None, None),
            P(("wide", "narrow"), None),
            P(("wide", "narrow")),
            P("wide"),
            P(),
            P(),
        ),
        out_specs=P(("wide", "narrow"), None),
        check_vma=False,
    )
```

```python
import functools

import jax
import jax.numpy as jnp
from jax import lax
from jax.experimental import pallas as pl
from jax.experimental.pallas import tpu as pltpu
from jax.sharding import PartitionSpec as P
MESH = pl.DeviceIdType.MESH


def _round_kernel(groups, per_block, slot_of_ref, slot_tile_ref, arrived_ref, tiles_ref,
                  degree_ref, w_in_ref, w_out_ref, out_ref,
                  parts, inbox, stage, edge_out, terms, send_a, recv_a, send_b, recv_b):
    me = lax.axis_index("narrow")
    col = lax.axis_index("wide")
    tile_count = tiles_ref.shape[0]
    barrier = pltpu.get_barrier_semaphore()
    for k in range(1, groups):
        pl.semaphore_signal(barrier, inc=1, device_id=(col, lax.rem(me + k, groups)), device_id_type=MESH)

    for e in range(tile_count // per_block):
        acc = None
        for k in range(per_block):
            t = e * per_block + k
            rows = arrived_ref[slot_of_ref[t]]
            p = jnp.dot(tiles_ref[t], rows, preferred_element_type=jnp.float32)
            acc = p if acc is None else acc + p
        parts[e] = acc

    pl.semaphore_wait(barrier, groups - 1)

    def first(d):
        return pltpu.make_async_remote_copy(
            src_ref=parts.at[d], dst_ref=inbox.at[me], send_sem=send_a.at[d],
            recv_sem=recv_a.at[me], device_id=(col, d), device_id_type=MESH)

    for k in range(1, groups):
        first(lax.rem(me + k, groups)).start()
    total = parts[me]
    for k in range(1, groups):
        d = lax.rem(me + k, groups)
        s = lax.rem(me + groups - k, groups)
        first(d).wait_send()
        pltpu.make_async_remote_copy(
            src_ref=parts.at[s], dst_ref=inbox.at[s], send_sem=send_a.at[s],
            recv_sem=recv_a.at[s], device_id=(col, s), device_id_type=MESH).wait_recv()
        total = total + inbox[s]
    edge_in = (total / degree_ref[...]).astype(jnp.bfloat16)
    pre = jnp.dot(edge_in, w_in_ref[...], preferred_element_type=jnp.float32)
    hidden = (pre * jax.nn.sigmoid(pre)).astype(jnp.bfloat16)
    own = jnp.dot(hidden, w_out_ref[...], preferred_element_type=jnp.float32).astype(jnp.bfloat16)
    stage[...] = own
    edge_out[me] = own

    def second(d):
        return pltpu.make_async_remote_copy(
            src_ref=stage, dst_ref=edge_out.at[me], send_sem=send_b.at[d],
            recv_sem=recv_b.at[me], device_id=(col, d), device_id_type=MESH)

    for k in range(1, groups):
        second(lax.rem(me + k, groups)).start()
    for k in range(1, groups):
        d = lax.rem(me + k, groups)
        s = lax.rem(me + groups - k, groups)
        second(d).wait_send()
        pltpu.make_async_remote_copy(
            src_ref=stage, dst_ref=edge_out.at[s], send_sem=send_b.at[s],
            recv_sem=recv_b.at[s], device_id=(col, s), device_id_type=MESH).wait_recv()

    for t in range(tile_count):
        term = lax.dot_general(
            tiles_ref[t], edge_out[t // per_block], (((0,), (0,)), ((), ())),
            preferred_element_type=jnp.float32)
        terms[t] = term.astype(jnp.bfloat16)

    def place(slot, carry):
        out_ref[slot] = terms[slot_tile_ref[slot]]
        return carry

    lax.fori_loop(0, out_ref.shape[0], place, 0)


def round_kernel(slot_of, slot_tile, arrived, tiles, degree, w_in, w_out, groups, per_block):
    slots, rows, channels = arrived.shape
    vmem = pl.BlockSpec(memory_space=pltpu.VMEM)
    smem = pl.BlockSpec(memory_space=pltpu.SMEM)
    return pl.pallas_call(
        functools.partial(_round_kernel, groups, per_block),
        out_shape=jax.ShapeDtypeStruct((slots, rows, channels), jnp.bfloat16),
        in_specs=[smem, smem] + [vmem] * 5,
        out_specs=vmem,
        scratch_shapes=[
            pltpu.VMEM((groups, rows, channels), jnp.float32),
            pltpu.VMEM((groups, rows, channels), jnp.float32),
            pltpu.VMEM((rows, channels), jnp.bfloat16),
            pltpu.VMEM((groups, rows, channels), jnp.bfloat16),
            pltpu.VMEM(tiles.shape, jnp.bfloat16),
            pltpu.SemaphoreType.DMA((groups,)), pltpu.SemaphoreType.DMA((groups,)),
            pltpu.SemaphoreType.DMA((groups,)), pltpu.SemaphoreType.DMA((groups,)),
        ],
        compiler_params=pltpu.CompilerParams(
            collective_id=0, has_side_effects=True, vmem_limit_bytes=48 * 1024 * 1024),
    )(slot_of, slot_tile, arrived, tiles, degree, w_in, w_out)


def edge_network(summed, degrees, w_in, w_out):
    edge_in = (summed / degrees.astype(jnp.float32)[:, None]).astype(jnp.bfloat16)
    pre_act = jnp.dot(edge_in, w_in, preferred_element_type=jnp.float32)
    hidden = jax.nn.silu(pre_act).astype(jnp.bfloat16)
    return jnp.dot(hidden, w_out, preferred_element_type=jnp.float32).astype(jnp.bfloat16)


def body(node_rows, tile_values, tile_owner, tile_block, edge_degree, w_in, w_out):
    owners = lax.axis_size("wide")
    tile_count, block_size, _ = tile_values.shape
    channels = node_rows.shape[1]
    node_block_count = node_rows.shape[0] // block_size
    edge_row_count = edge_degree.shape[0]
    edge_blocks = edge_row_count // block_size
    per_block = tile_count // edge_blocks
    capacity = max(2, 2 * tile_count // owners)
    slot_count = owners * capacity
    target = tile_owner[:, 0]
    positions = jnp.arange(tile_count, dtype=jnp.int32)
    earlier = (target[:, None] == target[None, :]) & (positions[None, :] < positions[:, None])
    order_in = jnp.sum(earlier.astype(jnp.int32), axis=1)
    slot_of = target * capacity + order_in
    slot_ids = jnp.arange(slot_count, dtype=jnp.int32)
    matches = slot_of[:, None] == slot_ids[None, :]
    wanted_out = jnp.sum(jnp.where(matches, tile_block[:, None] + 1, 0), axis=0) - 1
    wanted = lax.all_to_all(
        wanted_out.reshape(owners, capacity), "wide", split_axis=0, concat_axis=0, tiled=True
    ).reshape(slot_count)
    block_ids = jnp.arange(node_block_count, dtype=jnp.int32)
    selector = (wanted[None, :] == block_ids[:, None]).astype(jnp.bfloat16)
    current = node_rows
    node_blocks = current.reshape(node_block_count, block_size, channels)
    picked = node_blocks[jnp.maximum(wanted, 0)]
    arrived = lax.all_to_all(
        picked.reshape(owners, capacity, block_size, channels),
        "wide",
        split_axis=0,
        concat_axis=0,
        tiled=True,
    )
    groups = lax.axis_size("narrow")
    me = lax.axis_index("narrow")
    own_rows = edge_row_count // groups
    own_degree = lax.dynamic_slice_in_dim(edge_degree, me * own_rows, own_rows)
    tile_of_slot = jnp.sum(jnp.where(matches, positions[:, None], 0), axis=0)
    outgoing = round_kernel(
        slot_of,
        tile_of_slot,
        arrived.reshape(slot_count, block_size, channels),
        tile_values,
        own_degree.astype(jnp.float32)[:, None],
        w_in,
        w_out,
        groups,
        per_block,
    )
    returned = lax.all_to_all(
        outgoing.reshape(owners, capacity, block_size, channels),
        "wide",
        split_axis=0,
        concat_axis=0,
        tiled=True,
    )
    gathered = jnp.dot(
        selector,
        returned.reshape(slot_count, block_size * channels),
        preferred_element_type=jnp.float32,
    )
    current = (
        current.astype(jnp.float32) + gathered.reshape(node_block_count * block_size, channels)
    ).astype(jnp.bfloat16)
    return current


def solution(mesh):
    return jax.shard_map(
        body,
        mesh=mesh,
        in_specs=(
            P(("wide", "narrow"), None),
            P(("wide", "narrow"), None, None),
            P(("wide", "narrow"), None),
            P(("wide", "narrow")),
            P("wide"),
            P(),
            P(),
        ),
        out_specs=P(("wide", "narrow"), None),
        check_vma=False,
    )
```

```python
import functools

import jax
import jax.numpy as jnp
from jax import lax
from jax.experimental import pallas as pl
from jax.experimental.pallas import tpu as pltpu
from jax.sharding import PartitionSpec as P
MESH = pl.DeviceIdType.MESH


def _round_kernel(groups, per_block, slot_of_ref, slot_tile_ref, arrived_ref, tiles_ref,
                  degree_ref, w_in_ref, w_out_ref, out_ref,
                  parts, inbox, stage, edge_out, terms, send_a, recv_a, send_b, recv_b):
    me = lax.axis_index("narrow")
    col = lax.axis_index("wide")
    tile_count = tiles_ref.shape[0]
    barrier = pltpu.get_barrier_semaphore()
    for k in range(1, groups):
        pl.semaphore_signal(barrier, inc=1, device_id=(col, lax.rem(me + k, groups)), device_id_type=MESH)

    for e in range(tile_count // per_block):
        acc = None
        for k in range(per_block):
            t = e * per_block + k
            rows = arrived_ref[slot_of_ref[t]]
            p = jnp.dot(tiles_ref[t], rows, preferred_element_type=jnp.float32)
            acc = p if acc is None else acc + p
        parts[e] = acc

    pl.semaphore_wait(barrier, groups - 1)

    def first(d):
        return pltpu.make_async_remote_copy(
            src_ref=parts.at[d], dst_ref=inbox.at[me], send_sem=send_a.at[d],
            recv_sem=recv_a.at[me], device_id=(col, d), device_id_type=MESH)

    for k in range(1, groups):
        first(lax.rem(me + k, groups)).start()
    total = parts[me]
    for k in range(1, groups):
        d = lax.rem(me + k, groups)
        s = lax.rem(me + groups - k, groups)
        first(d).wait_send()
        pltpu.make_async_remote_copy(
            src_ref=parts.at[s], dst_ref=inbox.at[s], send_sem=send_a.at[s],
            recv_sem=recv_a.at[s], device_id=(col, s), device_id_type=MESH).wait_recv()
        total = total + inbox[s]
    edge_in = (total / degree_ref[...]).astype(jnp.bfloat16)
    pre = jnp.dot(edge_in, w_in_ref[...], preferred_element_type=jnp.float32)
    hidden = (pre * jax.nn.sigmoid(pre)).astype(jnp.bfloat16)
    own = jnp.dot(hidden, w_out_ref[...], preferred_element_type=jnp.float32).astype(jnp.bfloat16)
    stage[...] = own
    edge_out[me] = own

    def second(d):
        return pltpu.make_async_remote_copy(
            src_ref=stage, dst_ref=edge_out.at[me], send_sem=send_b.at[d],
            recv_sem=recv_b.at[me], device_id=(col, d), device_id_type=MESH)

    for k in range(1, groups):
        second(lax.rem(me + k, groups)).start()
    for k in range(1, groups):
        d = lax.rem(me + k, groups)
        s = lax.rem(me + groups - k, groups)
        second(d).wait_send()
        pltpu.make_async_remote_copy(
            src_ref=stage, dst_ref=edge_out.at[s], send_sem=send_b.at[s],
            recv_sem=recv_b.at[s], device_id=(col, s), device_id_type=MESH).wait_recv()

    for t in range(tile_count):
        term = lax.dot_general(
            tiles_ref[t], edge_out[t // per_block], (((0,), (0,)), ((), ())),
            preferred_element_type=jnp.float32)
        terms[t] = term.astype(jnp.bfloat16)

    def place(slot, carry):
        out_ref[slot] = terms[slot_tile_ref[slot]]
        return carry

    lax.fori_loop(0, out_ref.shape[0], place, 0)


def round_kernel(slot_of, slot_tile, arrived, tiles, degree, w_in, w_out, groups, per_block):
    slots, rows, channels = arrived.shape
    vmem = pl.BlockSpec(memory_space=pltpu.VMEM)
    smem = pl.BlockSpec(memory_space=pltpu.SMEM)
    return pl.pallas_call(
        functools.partial(_round_kernel, groups, per_block),
        out_shape=jax.ShapeDtypeStruct((slots, rows, channels), jnp.bfloat16),
        in_specs=[smem, smem] + [vmem] * 5,
        out_specs=vmem,
        scratch_shapes=[
            pltpu.VMEM((groups, rows, channels), jnp.float32),
            pltpu.VMEM((groups, rows, channels), jnp.float32),
            pltpu.VMEM((rows, channels), jnp.bfloat16),
            pltpu.VMEM((groups, rows, channels), jnp.bfloat16),
            pltpu.VMEM(tiles.shape, jnp.bfloat16),
            pltpu.SemaphoreType.DMA((groups,)), pltpu.SemaphoreType.DMA((groups,)),
            pltpu.SemaphoreType.DMA((groups,)), pltpu.SemaphoreType.DMA((groups,)),
        ],
        compiler_params=pltpu.CompilerParams(
            collective_id=0, has_side_effects=True, vmem_limit_bytes=48 * 1024 * 1024),
    )(slot_of, slot_tile, arrived, tiles, degree, w_in, w_out)


def _pick_kernel(wanted_ref, rows_ref, out_ref, sems):
    last = rows_ref.shape[0] - 1

    def copy(slot):
        block = jnp.minimum(wanted_ref[slot], last)
        return pltpu.make_async_copy(rows_ref.at[block], out_ref.at[slot], sems.at[slot])

    def start(slot, carry):
        @pl.when(wanted_ref[slot] >= 0)
        def _():
            copy(slot).start()

        return carry

    def finish(slot, carry):
        @pl.when(wanted_ref[slot] >= 0)
        def _():
            copy(slot).wait()

        return carry

    lax.fori_loop(0, out_ref.shape[0], start, 0)
    lax.fori_loop(0, out_ref.shape[0], finish, 0)


def pick_rows(wanted, blocks):
    slots = wanted.shape[0]
    _, rows, channels = blocks.shape
    return pl.pallas_call(
        _pick_kernel,
        out_shape=jax.ShapeDtypeStruct((slots, rows, channels), blocks.dtype),
        in_specs=[pl.BlockSpec(memory_space=pltpu.SMEM), pl.BlockSpec(memory_space=pltpu.VMEM)],
        out_specs=pl.BlockSpec(memory_space=pl.ANY),
        scratch_shapes=[pltpu.SemaphoreType.DMA((slots,))],
    )(wanted, blocks)


def _land_kernel(wanted_ref, returned_ref, rows_ref, out_ref, buf, acc, sems):
    last = rows_ref.shape[0] - 1

    def copy(slot):
        return pltpu.make_async_copy(returned_ref.at[slot], buf.at[slot], sems.at[slot])

    def start(slot, carry):
        @pl.when(wanted_ref[slot] >= 0)
        def _():
            copy(slot).start()

        return carry

    lax.fori_loop(0, buf.shape[0], start, 0)
    acc[...] = rows_ref[...].astype(jnp.float32)

    def add(slot, carry):
        @pl.when(wanted_ref[slot] >= 0)
        def _():
            copy(slot).wait()
            block = jnp.minimum(wanted_ref[slot], last)
            acc[block] = acc[block] + buf[slot].astype(jnp.float32)

        return carry

    lax.fori_loop(0, buf.shape[0], add, 0)
    out_ref[...] = acc[...].astype(out_ref.dtype)


def land_terms(wanted, returned, blocks):
    slots, rows, channels = returned.shape
    return pl.pallas_call(
        _land_kernel,
        out_shape=jax.ShapeDtypeStruct(blocks.shape, blocks.dtype),
        in_specs=[
            pl.BlockSpec(memory_space=pltpu.SMEM),
            pl.BlockSpec(memory_space=pl.ANY),
            pl.BlockSpec(memory_space=pltpu.VMEM),
        ],
        out_specs=pl.BlockSpec(memory_space=pltpu.VMEM),
        scratch_shapes=[
            pltpu.VMEM((slots, rows, channels), returned.dtype),
            pltpu.VMEM(blocks.shape, jnp.float32),
            pltpu.SemaphoreType.DMA((slots,)),
        ],
    )(wanted, returned, blocks)


def edge_network(summed, degrees, w_in, w_out):
    edge_in = (summed / degrees.astype(jnp.float32)[:, None]).astype(jnp.bfloat16)
    pre_act = jnp.dot(edge_in, w_in, preferred_element_type=jnp.float32)
    hidden = jax.nn.silu(pre_act).astype(jnp.bfloat16)
    return jnp.dot(hidden, w_out, preferred_element_type=jnp.float32).astype(jnp.bfloat16)


def body(node_rows, tile_values, tile_owner, tile_block, edge_degree, w_in, w_out):
    owners = lax.axis_size("wide")
    tile_count, block_size, _ = tile_values.shape
    channels = node_rows.shape[1]
    node_block_count = node_rows.shape[0] // block_size
    edge_row_count = edge_degree.shape[0]
    edge_blocks = edge_row_count // block_size
    per_block = tile_count // edge_blocks
    capacity = max(2, 2 * tile_count // owners)
    slot_count = owners * capacity
    target = tile_owner[:, 0]
    positions = jnp.arange(tile_count, dtype=jnp.int32)
    earlier = (target[:, None] == target[None, :]) & (positions[None, :] < positions[:, None])
    order_in = jnp.sum(earlier.astype(jnp.int32), axis=1)
    slot_of = target * capacity + order_in
    slot_ids = jnp.arange(slot_count, dtype=jnp.int32)
    matches = slot_of[:, None] == slot_ids[None, :]
    wanted_out = jnp.sum(jnp.where(matches, tile_block[:, None] + 1, 0), axis=0) - 1
    wanted = lax.all_to_all(
        wanted_out.reshape(owners, capacity), "wide", split_axis=0, concat_axis=0, tiled=True
    ).reshape(slot_count)
    current = node_rows
    node_blocks = current.reshape(node_block_count, block_size, channels)
    picked = pick_rows(wanted, node_blocks)
    arrived = lax.all_to_all(
        picked.reshape(owners, capacity, block_size, channels),
        "wide",
        split_axis=0,
        concat_axis=0,
        tiled=True,
    )
    groups = lax.axis_size("narrow")
    me = lax.axis_index("narrow")
    own_rows = edge_row_count // groups
    own_degree = lax.dynamic_slice_in_dim(edge_degree, me * own_rows, own_rows)
    tile_of_slot = jnp.sum(jnp.where(matches, positions[:, None], 0), axis=0)
    outgoing = round_kernel(
        slot_of,
        tile_of_slot,
        arrived.reshape(slot_count, block_size, channels),
        tile_values,
        own_degree.astype(jnp.float32)[:, None],
        w_in,
        w_out,
        groups,
        per_block,
    )
    returned = lax.all_to_all(
        outgoing.reshape(owners, capacity, block_size, channels),
        "wide",
        split_axis=0,
        concat_axis=0,
        tiled=True,
    )
    current = land_terms(
        wanted, returned.reshape(slot_count, block_size, channels), node_blocks
    ).reshape(node_block_count * block_size, channels)
    return current


def solution(mesh):
    return jax.shard_map(
        body,
        mesh=mesh,
        in_specs=(
            P(("wide", "narrow"), None),
            P(("wide", "narrow"), None, None),
            P(("wide", "narrow"), None),
            P(("wide", "narrow")),
            P("wide"),
            P(),
            P(),
        ),
        out_specs=P(("wide", "narrow"), None),
        check_vma=False,
    )
```

```python
import functools

import jax
import jax.numpy as jnp
from jax import lax
from jax.experimental import pallas as pl
from jax.experimental.pallas import tpu as pltpu
from jax.sharding import PartitionSpec as P
MESH = pl.DeviceIdType.MESH


def _round_kernel(groups, per_block, slot_of_ref, slot_tile_ref, arrived_ref, tiles_ref,
                  degree_ref, w_in_ref, w_out_ref, out_ref,
                  parts, inbox, stage, edge_out, terms, send_a, recv_a, send_b, recv_b):
    me = lax.axis_index("narrow")
    col = lax.axis_index("wide")
    tile_count = tiles_ref.shape[0]
    barrier = pltpu.get_barrier_semaphore()
    for k in range(1, groups):
        pl.semaphore_signal(barrier, inc=1, device_id=(col, lax.rem(me + k, groups)), device_id_type=MESH)

    for e in range(tile_count // per_block):
        acc = None
        for k in range(per_block):
            t = e * per_block + k
            rows = arrived_ref[slot_of_ref[t]]
            p = jnp.dot(tiles_ref[t], rows, preferred_element_type=jnp.float32)
            acc = p if acc is None else acc + p
        parts[e] = acc

    pl.semaphore_wait(barrier, groups - 1)

    def first(d):
        return pltpu.make_async_remote_copy(
            src_ref=parts.at[d], dst_ref=inbox.at[me], send_sem=send_a.at[d],
            recv_sem=recv_a.at[me], device_id=(col, d), device_id_type=MESH)

    for k in range(1, groups):
        first(lax.rem(me + k, groups)).start()
    total = parts[me]
    for k in range(1, groups):
        d = lax.rem(me + k, groups)
        s = lax.rem(me + groups - k, groups)
        first(d).wait_send()
        pltpu.make_async_remote_copy(
            src_ref=parts.at[s], dst_ref=inbox.at[s], send_sem=send_a.at[s],
            recv_sem=recv_a.at[s], device_id=(col, s), device_id_type=MESH).wait_recv()
        total = total + inbox[s]
    edge_in = (total / degree_ref[...]).astype(jnp.bfloat16)
    pre = jnp.dot(edge_in, w_in_ref[...], preferred_element_type=jnp.float32)
    hidden = (pre * jax.nn.sigmoid(pre)).astype(jnp.bfloat16)
    own = jnp.dot(hidden, w_out_ref[...], preferred_element_type=jnp.float32).astype(jnp.bfloat16)
    stage[...] = own
    edge_out[me] = own

    def second(d):
        return pltpu.make_async_remote_copy(
            src_ref=stage, dst_ref=edge_out.at[me], send_sem=send_b.at[d],
            recv_sem=recv_b.at[me], device_id=(col, d), device_id_type=MESH)

    for k in range(1, groups):
        second(lax.rem(me + k, groups)).start()
    for k in range(1, groups):
        d = lax.rem(me + k, groups)
        s = lax.rem(me + groups - k, groups)
        second(d).wait_send()
        pltpu.make_async_remote_copy(
            src_ref=stage, dst_ref=edge_out.at[s], send_sem=send_b.at[s],
            recv_sem=recv_b.at[s], device_id=(col, s), device_id_type=MESH).wait_recv()

    for t in range(tile_count):
        term = lax.dot_general(
            tiles_ref[t], edge_out[t // per_block], (((0,), (0,)), ((), ())),
            preferred_element_type=jnp.float32)
        terms[t] = term.astype(jnp.bfloat16)

    def place(slot, carry):
        out_ref[slot] = terms[slot_tile_ref[slot]]
        return carry

    lax.fori_loop(0, out_ref.shape[0], place, 0)


def round_kernel(slot_of, slot_tile, arrived, tiles, degree, w_in, w_out, groups, per_block):
    slots, rows, channels = arrived.shape
    vmem = pl.BlockSpec(memory_space=pltpu.VMEM)
    smem = pl.BlockSpec(memory_space=pltpu.SMEM)
    return pl.pallas_call(
        functools.partial(_round_kernel, groups, per_block),
        out_shape=jax.ShapeDtypeStruct((slots, rows, channels), jnp.bfloat16),
        in_specs=[smem, smem] + [vmem] * 5,
        out_specs=vmem,
        scratch_shapes=[
            pltpu.VMEM((groups, rows, channels), jnp.float32),
            pltpu.VMEM((groups, rows, channels), jnp.float32),
            pltpu.VMEM((rows, channels), jnp.bfloat16),
            pltpu.VMEM((groups, rows, channels), jnp.bfloat16),
            pltpu.VMEM(tiles.shape, jnp.bfloat16),
            pltpu.SemaphoreType.DMA((groups,)), pltpu.SemaphoreType.DMA((groups,)),
            pltpu.SemaphoreType.DMA((groups,)), pltpu.SemaphoreType.DMA((groups,)),
        ],
        compiler_params=pltpu.CompilerParams(
            collective_id=0, has_side_effects=True, vmem_limit_bytes=48 * 1024 * 1024),
    )(slot_of, slot_tile, arrived, tiles, degree, w_in, w_out)


def _pick_kernel(wanted_ref, rows_ref, out_ref, sems):
    last = rows_ref.shape[0] - 1

    def copy(slot):
        block = jnp.minimum(wanted_ref[slot], last)
        return pltpu.make_async_copy(rows_ref.at[block], out_ref.at[slot], sems.at[slot])

    def start(slot, carry):
        @pl.when(wanted_ref[slot] >= 0)
        def _():
            copy(slot).start()

        return carry

    def finish(slot, carry):
        @pl.when(wanted_ref[slot] >= 0)
        def _():
            copy(slot).wait()

        return carry

    lax.fori_loop(0, out_ref.shape[0], start, 0)
    lax.fori_loop(0, out_ref.shape[0], finish, 0)


def pick_rows(wanted, blocks):
    slots = wanted.shape[0]
    _, rows, channels = blocks.shape
    return pl.pallas_call(
        _pick_kernel,
        out_shape=jax.ShapeDtypeStruct((slots, rows, channels), blocks.dtype),
        in_specs=[pl.BlockSpec(memory_space=pltpu.SMEM), pl.BlockSpec(memory_space=pltpu.VMEM)],
        out_specs=pl.BlockSpec(memory_space=pl.ANY),
        scratch_shapes=[pltpu.SemaphoreType.DMA((slots,))],
    )(wanted, blocks)


def _land_kernel(wanted_ref, returned_ref, rows_ref, out_ref, buf, acc, sems):
    last = rows_ref.shape[0] - 1

    def copy(slot):
        return pltpu.make_async_copy(returned_ref.at[slot], buf.at[slot], sems.at[slot])

    def start(slot, carry):
        @pl.when(wanted_ref[slot] >= 0)
        def _():
            copy(slot).start()

        return carry

    lax.fori_loop(0, buf.shape[0], start, 0)
    acc[...] = rows_ref[...].astype(jnp.float32)

    def add(slot, carry):
        @pl.when(wanted_ref[slot] >= 0)
        def _():
            copy(slot).wait()
            block = jnp.minimum(wanted_ref[slot], last)
            acc[block] = acc[block] + buf[slot].astype(jnp.float32)

        return carry

    lax.fori_loop(0, buf.shape[0], add, 0)
    out_ref[...] = acc[...].astype(out_ref.dtype)


def land_terms(wanted, returned, blocks):
    slots, rows, channels = returned.shape
    return pl.pallas_call(
        _land_kernel,
        out_shape=jax.ShapeDtypeStruct(blocks.shape, blocks.dtype),
        in_specs=[
            pl.BlockSpec(memory_space=pltpu.SMEM),
            pl.BlockSpec(memory_space=pl.ANY),
            pl.BlockSpec(memory_space=pltpu.VMEM),
        ],
        out_specs=pl.BlockSpec(memory_space=pltpu.VMEM),
        scratch_shapes=[
            pltpu.VMEM((slots, rows, channels), returned.dtype),
            pltpu.VMEM(blocks.shape, jnp.float32),
            pltpu.SemaphoreType.DMA((slots,)),
        ],
    )(wanted, returned, blocks)


def edge_network(summed, degrees, w_in, w_out):
    edge_in = (summed / degrees.astype(jnp.float32)[:, None]).astype(jnp.bfloat16)
    pre_act = jnp.dot(edge_in, w_in, preferred_element_type=jnp.float32)
    hidden = jax.nn.silu(pre_act).astype(jnp.bfloat16)
    return jnp.dot(hidden, w_out, preferred_element_type=jnp.float32).astype(jnp.bfloat16)


def body(node_rows, tile_values, tile_owner, tile_block, edge_degree, w_in, w_out):
    owners = lax.axis_size("wide")
    tile_count, block_size, _ = tile_values.shape
    channels = node_rows.shape[1]
    node_block_count = node_rows.shape[0] // block_size
    edge_row_count = edge_degree.shape[0]
    edge_blocks = edge_row_count // block_size
    per_block = tile_count // edge_blocks
    capacity = max(2, 2 * tile_count // owners)
    slot_count = owners * capacity
    target = tile_owner[:, 0]
    positions = jnp.arange(tile_count, dtype=jnp.int32)
    earlier = (target[:, None] == target[None, :]) & (positions[None, :] < positions[:, None])
    order_in = jnp.sum(earlier.astype(jnp.int32), axis=1)
    slot_of = target * capacity + order_in
    slot_ids = jnp.arange(slot_count, dtype=jnp.int32)
    matches = slot_of[:, None] == slot_ids[None, :]
    wanted_out = jnp.sum(jnp.where(matches, tile_block[:, None] + 1, 0), axis=0) - 1
    groups = lax.axis_size("narrow")
    me = lax.axis_index("narrow")
    own_rows = edge_row_count // groups
    own_degree = lax.dynamic_slice_in_dim(edge_degree, me * own_rows, own_rows)
    tile_of_slot = jnp.sum(jnp.where(matches, positions[:, None], 0), axis=0)
    wanted = lax.all_to_all(
        wanted_out.reshape(owners, capacity), "wide", split_axis=0, concat_axis=0, tiled=True
    ).reshape(slot_count)
    current = node_rows
    node_blocks = current.reshape(node_block_count, block_size, channels)
    degree_column = jnp.broadcast_to(own_degree.astype(jnp.float32)[:, None], (own_rows, channels))
    wanted, slot_of, tile_of_slot, degree_column = lax.optimization_barrier(
        (wanted, slot_of, tile_of_slot, degree_column)
    )
    picked = pick_rows(wanted, node_blocks)
    arrived = lax.all_to_all(
        picked.reshape(owners, capacity, block_size, channels),
        "wide",
        split_axis=0,
        concat_axis=0,
        tiled=True,
    )
    outgoing = round_kernel(
        slot_of,
        tile_of_slot,
        arrived.reshape(slot_count, block_size, channels),
        tile_values,
        degree_column,
        w_in,
        w_out,
        groups,
        per_block,
    )
    returned = lax.all_to_all(
        outgoing.reshape(owners, capacity, block_size, channels),
        "wide",
        split_axis=0,
        concat_axis=0,
        tiled=True,
    )
    current = land_terms(
        wanted, returned.reshape(slot_count, block_size, channels), node_blocks
    ).reshape(node_block_count * block_size, channels)
    return current


def solution(mesh):
    return jax.shard_map(
        body,
        mesh=mesh,
        in_specs=(
            P(("wide", "narrow"), None),
            P(("wide", "narrow"), None, None),
            P(("wide", "narrow"), None),
            P(("wide", "narrow")),
            P("wide"),
            P(),
            P(),
        ),
        out_specs=P(("wide", "narrow"), None),
        check_vma=False,
    )
```

```python
import functools

import jax
import jax.numpy as jnp
from jax import lax
from jax.experimental import pallas as pl
from jax.experimental.pallas import tpu as pltpu
from jax.sharding import PartitionSpec as P
MESH = pl.DeviceIdType.MESH


def _round_kernel(groups, per_block, slot_of_ref, slot_tile_ref, arrived_ref, tiles_ref,
                  degree_ref, w_in_ref, w_out_ref, out_ref,
                  parts, inbox, stage, edge_out, terms, send_a, recv_a, send_b, recv_b,
                  placed, flush_sem):
    me = lax.axis_index("narrow")
    col = lax.axis_index("wide")
    tile_count = tiles_ref.shape[0]
    barrier = pltpu.get_barrier_semaphore()
    for k in range(1, groups):
        pl.semaphore_signal(barrier, inc=1, device_id=(col, lax.rem(me + k, groups)), device_id_type=MESH)

    for e in range(tile_count // per_block):
        acc = None
        for k in range(per_block):
            t = e * per_block + k
            rows = arrived_ref[slot_of_ref[t]]
            p = jnp.dot(tiles_ref[t], rows, preferred_element_type=jnp.float32)
            acc = p if acc is None else acc + p
        parts[e] = acc

    pl.semaphore_wait(barrier, groups - 1)

    def first(d):
        return pltpu.make_async_remote_copy(
            src_ref=parts.at[d], dst_ref=inbox.at[me], send_sem=send_a.at[d],
            recv_sem=recv_a.at[me], device_id=(col, d), device_id_type=MESH)

    for k in range(1, groups):
        first(lax.rem(me + k, groups)).start()
    total = parts[me]
    for k in range(1, groups):
        d = lax.rem(me + k, groups)
        s = lax.rem(me + groups - k, groups)
        first(d).wait_send()
        pltpu.make_async_remote_copy(
            src_ref=parts.at[s], dst_ref=inbox.at[s], send_sem=send_a.at[s],
            recv_sem=recv_a.at[s], device_id=(col, s), device_id_type=MESH).wait_recv()
        total = total + inbox[s]
    edge_in = (total / degree_ref[...]).astype(jnp.bfloat16)
    pre = jnp.dot(edge_in, w_in_ref[...], preferred_element_type=jnp.float32)
    hidden = (pre * jax.nn.sigmoid(pre)).astype(jnp.bfloat16)
    own = jnp.dot(hidden, w_out_ref[...], preferred_element_type=jnp.float32).astype(jnp.bfloat16)
    stage[...] = own
    edge_out[me] = own

    def second(d):
        return pltpu.make_async_remote_copy(
            src_ref=stage, dst_ref=edge_out.at[me], send_sem=send_b.at[d],
            recv_sem=recv_b.at[me], device_id=(col, d), device_id_type=MESH)

    for k in range(1, groups):
        second(lax.rem(me + k, groups)).start()
    for k in range(1, groups):
        d = lax.rem(me + k, groups)
        s = lax.rem(me + groups - k, groups)
        second(d).wait_send()
        pltpu.make_async_remote_copy(
            src_ref=stage, dst_ref=edge_out.at[s], send_sem=send_b.at[s],
            recv_sem=recv_b.at[s], device_id=(col, s), device_id_type=MESH).wait_recv()

    for t in range(tile_count):
        term = lax.dot_general(
            tiles_ref[t], edge_out[t // per_block], (((0,), (0,)), ((), ())),
            preferred_element_type=jnp.float32)
        terms[t] = term.astype(jnp.bfloat16)

    def place(slot, carry):
        placed[slot] = terms[slot_tile_ref[slot]]
        return carry

    lax.fori_loop(0, out_ref.shape[0], place, 0)
    flush = pltpu.make_async_copy(placed, out_ref, flush_sem)
    flush.start()
    flush.wait()


def round_kernel(slot_of, slot_tile, arrived, tiles, degree, w_in, w_out, groups, per_block):
    slots, rows, channels = arrived.shape
    vmem = pl.BlockSpec(memory_space=pltpu.VMEM)
    smem = pl.BlockSpec(memory_space=pltpu.SMEM)
    return pl.pallas_call(
        functools.partial(_round_kernel, groups, per_block),
        out_shape=jax.ShapeDtypeStruct((slots, rows, channels), jnp.bfloat16),
        in_specs=[smem, smem] + [vmem] * 5,
        out_specs=pl.BlockSpec(memory_space=pltpu.HBM),
        scratch_shapes=[
            pltpu.VMEM((groups, rows, channels), jnp.float32),
            pltpu.VMEM((groups, rows, channels), jnp.float32),
            pltpu.VMEM((rows, channels), jnp.bfloat16),
            pltpu.VMEM((groups, rows, channels), jnp.bfloat16),
            pltpu.VMEM(tiles.shape, jnp.bfloat16),
            pltpu.SemaphoreType.DMA((groups,)), pltpu.SemaphoreType.DMA((groups,)),
            pltpu.SemaphoreType.DMA((groups,)), pltpu.SemaphoreType.DMA((groups,)),
            pltpu.VMEM((slots, rows, channels), jnp.bfloat16),
            pltpu.SemaphoreType.DMA,
        ],
        compiler_params=pltpu.CompilerParams(
            collective_id=0, has_side_effects=True, vmem_limit_bytes=67043328),
    )(slot_of, slot_tile, arrived, tiles, degree, w_in, w_out)


def _pick_kernel(wanted_ref, rows_ref, out_ref, sems):
    last = rows_ref.shape[0] - 1

    def copy(slot):
        block = jnp.minimum(wanted_ref[slot], last)
        return pltpu.make_async_copy(rows_ref.at[block], out_ref.at[slot], sems.at[slot])

    def start(slot, carry):
        @pl.when(wanted_ref[slot] >= 0)
        def _():
            copy(slot).start()

        return carry

    def finish(slot, carry):
        @pl.when(wanted_ref[slot] >= 0)
        def _():
            copy(slot).wait()

        return carry

    lax.fori_loop(0, out_ref.shape[0], start, 0)
    lax.fori_loop(0, out_ref.shape[0], finish, 0)


def pick_rows(wanted, blocks):
    slots = wanted.shape[0]
    _, rows, channels = blocks.shape
    return pl.pallas_call(
        _pick_kernel,
        out_shape=jax.ShapeDtypeStruct((slots, rows, channels), blocks.dtype),
        in_specs=[pl.BlockSpec(memory_space=pltpu.SMEM), pl.BlockSpec(memory_space=pltpu.VMEM)],
        out_specs=pl.BlockSpec(memory_space=pl.ANY),
        scratch_shapes=[pltpu.SemaphoreType.DMA((slots,))],
    )(wanted, blocks)


def _land_kernel(wanted_ref, returned_ref, rows_ref, out_ref, buf, acc, sems):
    last = rows_ref.shape[0] - 1

    def copy(slot):
        return pltpu.make_async_copy(returned_ref.at[slot], buf.at[slot], sems.at[slot])

    def start(slot, carry):
        @pl.when(wanted_ref[slot] >= 0)
        def _():
            copy(slot).start()

        return carry

    lax.fori_loop(0, buf.shape[0], start, 0)
    acc[...] = rows_ref[...].astype(jnp.float32)

    def add(slot, carry):
        @pl.when(wanted_ref[slot] >= 0)
        def _():
            copy(slot).wait()
            block = jnp.minimum(wanted_ref[slot], last)
            acc[block] = acc[block] + buf[slot].astype(jnp.float32)

        return carry

    lax.fori_loop(0, buf.shape[0], add, 0)
    out_ref[...] = acc[...].astype(out_ref.dtype)


def land_terms(wanted, returned, blocks):
    slots, rows, channels = returned.shape
    return pl.pallas_call(
        _land_kernel,
        out_shape=jax.ShapeDtypeStruct(blocks.shape, blocks.dtype),
        in_specs=[
            pl.BlockSpec(memory_space=pltpu.SMEM),
            pl.BlockSpec(memory_space=pl.ANY),
            pl.BlockSpec(memory_space=pltpu.VMEM),
        ],
        out_specs=pl.BlockSpec(memory_space=pltpu.VMEM),
        scratch_shapes=[
            pltpu.VMEM((slots, rows, channels), returned.dtype),
            pltpu.VMEM(blocks.shape, jnp.float32),
            pltpu.SemaphoreType.DMA((slots,)),
        ],
    )(wanted, returned, blocks)


def edge_network(summed, degrees, w_in, w_out):
    edge_in = (summed / degrees.astype(jnp.float32)[:, None]).astype(jnp.bfloat16)
    pre_act = jnp.dot(edge_in, w_in, preferred_element_type=jnp.float32)
    hidden = jax.nn.silu(pre_act).astype(jnp.bfloat16)
    return jnp.dot(hidden, w_out, preferred_element_type=jnp.float32).astype(jnp.bfloat16)


def body(node_rows, tile_values, tile_owner, tile_block, edge_degree, w_in, w_out):
    owners = lax.axis_size("wide")
    tile_count, block_size, _ = tile_values.shape
    channels = node_rows.shape[1]
    node_block_count = node_rows.shape[0] // block_size
    edge_row_count = edge_degree.shape[0]
    edge_blocks = edge_row_count // block_size
    per_block = tile_count // edge_blocks
    capacity = max(2, 2 * tile_count // owners)
    slot_count = owners * capacity
    target = tile_owner[:, 0]
    positions = jnp.arange(tile_count, dtype=jnp.int32)
    earlier = (target[:, None] == target[None, :]) & (positions[None, :] < positions[:, None])
    order_in = jnp.sum(earlier.astype(jnp.int32), axis=1)
    slot_of = target * capacity + order_in
    slot_ids = jnp.arange(slot_count, dtype=jnp.int32)
    matches = slot_of[:, None] == slot_ids[None, :]
    wanted_out = jnp.sum(jnp.where(matches, tile_block[:, None] + 1, 0), axis=0) - 1
    groups = lax.axis_size("narrow")
    me = lax.axis_index("narrow")
    own_rows = edge_row_count // groups
    own_degree = lax.dynamic_slice_in_dim(edge_degree, me * own_rows, own_rows)
    tile_of_slot = jnp.sum(jnp.where(matches, positions[:, None], 0), axis=0)
    wanted = lax.all_to_all(
        wanted_out.reshape(owners, capacity), "wide", split_axis=0, concat_axis=0, tiled=True
    ).reshape(slot_count)
    current = node_rows
    node_blocks = current.reshape(node_block_count, block_size, channels)
    degree_column = jnp.broadcast_to(own_degree.astype(jnp.float32)[:, None], (own_rows, channels))
    wanted, slot_of, tile_of_slot, degree_column = lax.optimization_barrier(
        (wanted, slot_of, tile_of_slot, degree_column)
    )
    picked = pick_rows(wanted, node_blocks)
    arrived = lax.all_to_all(
        picked.reshape(owners, capacity, block_size, channels),
        "wide",
        split_axis=0,
        concat_axis=0,
        tiled=True,
    )
    outgoing = round_kernel(
        slot_of,
        tile_of_slot,
        arrived.reshape(slot_count, block_size, channels),
        tile_values,
        degree_column,
        w_in,
        w_out,
        groups,
        per_block,
    )
    returned = lax.all_to_all(
        outgoing.reshape(owners, capacity, block_size, channels),
        "wide",
        split_axis=0,
        concat_axis=0,
        tiled=True,
    )
    current = land_terms(
        wanted, returned.reshape(slot_count, block_size, channels), node_blocks
    ).reshape(node_block_count * block_size, channels)
    return current


def solution(mesh):
    return jax.shard_map(
        body,
        mesh=mesh,
        in_specs=(
            P(("wide", "narrow"), None),
            P(("wide", "narrow"), None, None),
            P(("wide", "narrow"), None),
            P(("wide", "narrow")),
            P("wide"),
            P(),
            P(),
        ),
        out_specs=P(("wide", "narrow"), None),
        check_vma=False,
    )
```

```python
import functools

import jax
import jax.numpy as jnp
from jax import lax
from jax.experimental import pallas as pl
from jax.experimental.pallas import tpu as pltpu
from jax.sharding import PartitionSpec as P
MESH = pl.DeviceIdType.MESH


def _round_kernel(groups, per_block, slot_of_ref, slot_tile_ref, arrived_ref, tiles_ref,
                  degree_ref, w_in_ref, w_out_ref, out_ref,
                  parts, inbox, stage, edge_out, terms, send_a, recv_a, send_b, recv_b):
    me = lax.axis_index("narrow")
    col = lax.axis_index("wide")
    tile_count = tiles_ref.shape[0]
    barrier = pltpu.get_barrier_semaphore()
    for k in range(1, groups):
        pl.semaphore_signal(barrier, inc=1, device_id=(col, lax.rem(me + k, groups)), device_id_type=MESH)

    for e in range(tile_count // per_block):
        acc = None
        for k in range(per_block):
            t = e * per_block + k
            rows = arrived_ref[slot_of_ref[t]]
            p = jnp.dot(tiles_ref[t], rows, preferred_element_type=jnp.float32)
            acc = p if acc is None else acc + p
        parts[e] = acc

    pl.semaphore_wait(barrier, groups - 1)

    def first(d):
        return pltpu.make_async_remote_copy(
            src_ref=parts.at[d], dst_ref=inbox.at[me], send_sem=send_a.at[d],
            recv_sem=recv_a.at[me], device_id=(col, d), device_id_type=MESH)

    for k in range(1, groups):
        first(lax.rem(me + k, groups)).start()
    total = parts[me]
    for k in range(1, groups):
        d = lax.rem(me + k, groups)
        s = lax.rem(me + groups - k, groups)
        first(d).wait_send()
        pltpu.make_async_remote_copy(
            src_ref=parts.at[s], dst_ref=inbox.at[s], send_sem=send_a.at[s],
            recv_sem=recv_a.at[s], device_id=(col, s), device_id_type=MESH).wait_recv()
        total = total + inbox[s]
    edge_in = (total / degree_ref[...]).astype(jnp.bfloat16)
    pre = jnp.dot(edge_in, w_in_ref[...], preferred_element_type=jnp.float32)
    hidden = (pre * jax.nn.sigmoid(pre)).astype(jnp.bfloat16)
    own = jnp.dot(hidden, w_out_ref[...], preferred_element_type=jnp.float32).astype(jnp.bfloat16)
    stage[...] = own
    edge_out[me] = own

    def second(d):
        return pltpu.make_async_remote_copy(
            src_ref=stage, dst_ref=edge_out.at[me], send_sem=send_b.at[d],
            recv_sem=recv_b.at[me], device_id=(col, d), device_id_type=MESH)

    for k in range(1, groups):
        second(lax.rem(me + k, groups)).start()
    for k in range(1, groups):
        d = lax.rem(me + k, groups)
        s = lax.rem(me + groups - k, groups)
        second(d).wait_send()
        pltpu.make_async_remote_copy(
            src_ref=stage, dst_ref=edge_out.at[s], send_sem=send_b.at[s],
            recv_sem=recv_b.at[s], device_id=(col, s), device_id_type=MESH).wait_recv()

    for t in range(tile_count):
        term = lax.dot_general(
            tiles_ref[t], edge_out[t // per_block], (((0,), (0,)), ((), ())),
            preferred_element_type=jnp.float32)
        terms[t] = term.astype(jnp.bfloat16)

    def place(slot, carry):
        out_ref[slot] = terms[slot_tile_ref[slot]]
        return carry

    lax.fori_loop(0, out_ref.shape[0], place, 0)


def round_kernel(slot_of, slot_tile, arrived, tiles, degree, w_in, w_out, groups, per_block):
    slots, rows, channels = arrived.shape
    vmem = pl.BlockSpec(memory_space=pltpu.VMEM)
    smem = pl.BlockSpec(memory_space=pltpu.SMEM)
    return pl.pallas_call(
        functools.partial(_round_kernel, groups, per_block),
        out_shape=jax.ShapeDtypeStruct((slots, rows, channels), jnp.bfloat16),
        in_specs=[smem, smem] + [vmem] * 5,
        out_specs=vmem,
        scratch_shapes=[
            pltpu.VMEM((groups, rows, channels), jnp.float32),
            pltpu.VMEM((groups, rows, channels), jnp.float32),
            pltpu.VMEM((rows, channels), jnp.bfloat16),
            pltpu.VMEM((groups, rows, channels), jnp.bfloat16),
            pltpu.VMEM(tiles.shape, jnp.bfloat16),
            pltpu.SemaphoreType.DMA((groups,)), pltpu.SemaphoreType.DMA((groups,)),
            pltpu.SemaphoreType.DMA((groups,)), pltpu.SemaphoreType.DMA((groups,)),
        ],
        compiler_params=pltpu.CompilerParams(
            collective_id=0, has_side_effects=True, vmem_limit_bytes=48 * 1024 * 1024),
    )(slot_of, slot_tile, arrived, tiles, degree, w_in, w_out)


def _pick_kernel(count_ref, order_ref, wanted_ref, rows_ref, out_ref, sems):
    last = rows_ref.shape[0] - 1

    def copy(i):
        slot = order_ref[i]
        block = jnp.clip(wanted_ref[slot], 0, last)
        return pltpu.make_async_copy(rows_ref.at[block], out_ref.at[slot], sems.at[i])

    def start(i, carry):
        copy(i).start()
        return carry

    def finish(i, carry):
        copy(i).wait()
        return carry

    lax.fori_loop(0, count_ref[0], start, 0)
    lax.fori_loop(0, count_ref[0], finish, 0)


def pick_rows(count, order, wanted, blocks):
    slots = wanted.shape[0]
    _, rows, channels = blocks.shape
    smem = pl.BlockSpec(memory_space=pltpu.SMEM)
    return pl.pallas_call(
        _pick_kernel,
        out_shape=jax.ShapeDtypeStruct((slots, rows, channels), blocks.dtype),
        in_specs=[smem, smem, smem, pl.BlockSpec(memory_space=pltpu.VMEM)],
        out_specs=pl.BlockSpec(memory_space=pl.ANY),
        scratch_shapes=[pltpu.SemaphoreType.DMA((slots,))],
    )(count, order, wanted, blocks)


def _land_kernel(count_ref, order_ref, wanted_ref, returned_ref, rows_ref, out_ref, buf, acc, sems):
    last = rows_ref.shape[0] - 1

    def copy(i):
        return pltpu.make_async_copy(returned_ref.at[order_ref[i]], buf.at[i], sems.at[i])

    def start(i, carry):
        copy(i).start()
        return carry

    lax.fori_loop(0, count_ref[0], start, 0)
    acc[...] = rows_ref[...].astype(jnp.float32)

    def add(i, carry):
        copy(i).wait()
        block = jnp.clip(wanted_ref[order_ref[i]], 0, last)
        acc[block] = acc[block] + buf[i].astype(jnp.float32)
        return carry

    lax.fori_loop(0, count_ref[0], add, 0)
    out_ref[...] = acc[...].astype(out_ref.dtype)


def land_terms(count, order, wanted, returned, blocks):
    slots, rows, channels = returned.shape
    smem = pl.BlockSpec(memory_space=pltpu.SMEM)
    return pl.pallas_call(
        _land_kernel,
        out_shape=jax.ShapeDtypeStruct(blocks.shape, blocks.dtype),
        in_specs=[smem, smem, smem, pl.BlockSpec(memory_space=pl.ANY), pl.BlockSpec(memory_space=pltpu.VMEM)],
        out_specs=pl.BlockSpec(memory_space=pltpu.VMEM),
        scratch_shapes=[
            pltpu.VMEM((slots, rows, channels), returned.dtype),
            pltpu.VMEM(blocks.shape, jnp.float32),
            pltpu.SemaphoreType.DMA((slots,)),
        ],
    )(count, order, wanted, returned, blocks)


def edge_network(summed, degrees, w_in, w_out):
    edge_in = (summed / degrees.astype(jnp.float32)[:, None]).astype(jnp.bfloat16)
    pre_act = jnp.dot(edge_in, w_in, preferred_element_type=jnp.float32)
    hidden = jax.nn.silu(pre_act).astype(jnp.bfloat16)
    return jnp.dot(hidden, w_out, preferred_element_type=jnp.float32).astype(jnp.bfloat16)


def body(node_rows, tile_values, tile_owner, tile_block, edge_degree, w_in, w_out):
    owners = lax.axis_size("wide")
    tile_count, block_size, _ = tile_values.shape
    channels = node_rows.shape[1]
    node_block_count = node_rows.shape[0] // block_size
    edge_row_count = edge_degree.shape[0]
    edge_blocks = edge_row_count // block_size
    per_block = tile_count // edge_blocks
    capacity = max(2, 2 * tile_count // owners)
    slot_count = owners * capacity
    target = tile_owner[:, 0]
    positions = jnp.arange(tile_count, dtype=jnp.int32)
    earlier = (target[:, None] == target[None, :]) & (positions[None, :] < positions[:, None])
    order_in = jnp.sum(earlier.astype(jnp.int32), axis=1)
    slot_of = target * capacity + order_in
    slot_ids = jnp.arange(slot_count, dtype=jnp.int32)
    matches = slot_of[:, None] == slot_ids[None, :]
    wanted_out = jnp.sum(jnp.where(matches, tile_block[:, None] + 1, 0), axis=0) - 1
    groups = lax.axis_size("narrow")
    me = lax.axis_index("narrow")
    own_rows = edge_row_count // groups
    own_degree = lax.dynamic_slice_in_dim(edge_degree, me * own_rows, own_rows)
    tile_of_slot = jnp.sum(jnp.where(matches, positions[:, None], 0), axis=0)
    wanted = lax.all_to_all(
        wanted_out.reshape(owners, capacity), "wide", split_axis=0, concat_axis=0, tiled=True
    ).reshape(slot_count)
    current = node_rows
    node_blocks = current.reshape(node_block_count, block_size, channels)
    degree_column = jnp.broadcast_to(own_degree.astype(jnp.float32)[:, None], (own_rows, channels))
    wanted, slot_of, tile_of_slot, degree_column = lax.optimization_barrier(
        (wanted, slot_of, tile_of_slot, degree_column)
    )
    filled = wanted >= 0
    rank = jnp.cumsum(filled.astype(jnp.int32)) - 1
    count = jnp.sum(filled.astype(jnp.int32)).reshape(1)
    order = jnp.sum(
        jnp.where(filled[None, :] & (rank[None, :] == slot_ids[:, None]), slot_ids[None, :], 0),
        axis=1,
    )
    picked = pick_rows(count, order, wanted, node_blocks)
    arrived = lax.all_to_all(
        picked.reshape(owners, capacity, block_size, channels),
        "wide",
        split_axis=0,
        concat_axis=0,
        tiled=True,
    )
    outgoing = round_kernel(
        slot_of,
        tile_of_slot,
        arrived.reshape(slot_count, block_size, channels),
        tile_values,
        degree_column,
        w_in,
        w_out,
        groups,
        per_block,
    )
    returned = lax.all_to_all(
        outgoing.reshape(owners, capacity, block_size, channels),
        "wide",
        split_axis=0,
        concat_axis=0,
        tiled=True,
    )
    current = land_terms(
        count, order, wanted, returned.reshape(slot_count, block_size, channels), node_blocks
    ).reshape(node_block_count * block_size, channels)
    return current


def solution(mesh):
    return jax.shard_map(
        body,
        mesh=mesh,
        in_specs=(
            P(("wide", "narrow"), None),
            P(("wide", "narrow"), None, None),
            P(("wide", "narrow"), None),
            P(("wide", "narrow")),
            P("wide"),
            P(),
            P(),
        ),
        out_specs=P(("wide", "narrow"), None),
        check_vma=False,
    )
```

```python
import functools

import jax
import jax.numpy as jnp
from jax import lax
from jax.experimental import pallas as pl
from jax.experimental.pallas import tpu as pltpu
from jax.sharding import PartitionSpec as P
MESH = pl.DeviceIdType.MESH


def _round_kernel(groups, per_block, slot_of_ref, slot_tile_ref, arrived_ref, tiles_ref,
                  degree_ref, w_in_ref, w_out_ref, out_ref,
                  parts, inbox, stage, edge_out, terms, send_a, recv_a, send_b, recv_b):
    me = lax.axis_index("narrow")
    col = lax.axis_index("wide")
    tile_count = tiles_ref.shape[0]
    barrier = pltpu.get_barrier_semaphore()
    for k in range(1, groups):
        pl.semaphore_signal(barrier, inc=1, device_id=(col, lax.rem(me + k, groups)), device_id_type=MESH)

    for e in range(tile_count // per_block):
        acc = None
        for k in range(per_block):
            t = e * per_block + k
            rows = arrived_ref[slot_of_ref[t]]
            p = jnp.dot(tiles_ref[t], rows, preferred_element_type=jnp.float32)
            acc = p if acc is None else acc + p
        parts[e] = acc

    pl.semaphore_wait(barrier, groups - 1)

    def first(d):
        return pltpu.make_async_remote_copy(
            src_ref=parts.at[d], dst_ref=inbox.at[me], send_sem=send_a.at[d],
            recv_sem=recv_a.at[me], device_id=(col, d), device_id_type=MESH)

    for k in range(1, groups):
        first(lax.rem(me + k, groups)).start()
    total = parts[me]
    for k in range(1, groups):
        d = lax.rem(me + k, groups)
        s = lax.rem(me + groups - k, groups)
        first(d).wait_send()
        pltpu.make_async_remote_copy(
            src_ref=parts.at[s], dst_ref=inbox.at[s], send_sem=send_a.at[s],
            recv_sem=recv_a.at[s], device_id=(col, s), device_id_type=MESH).wait_recv()
        total = total + inbox[s]
    edge_in = (total / degree_ref[...]).astype(jnp.bfloat16)
    pre = jnp.dot(edge_in, w_in_ref[...], preferred_element_type=jnp.float32)
    hidden = (pre * jax.nn.sigmoid(pre)).astype(jnp.bfloat16)
    own = jnp.dot(hidden, w_out_ref[...], preferred_element_type=jnp.float32).astype(jnp.bfloat16)
    stage[...] = own
    edge_out[me] = own

    def second(d):
        return pltpu.make_async_remote_copy(
            src_ref=stage, dst_ref=edge_out.at[me], send_sem=send_b.at[d],
            recv_sem=recv_b.at[me], device_id=(col, d), device_id_type=MESH)

    for k in range(1, groups):
        second(lax.rem(me + k, groups)).start()
    for k in range(1, groups):
        d = lax.rem(me + k, groups)
        s = lax.rem(me + groups - k, groups)
        second(d).wait_send()
        pltpu.make_async_remote_copy(
            src_ref=stage, dst_ref=edge_out.at[s], send_sem=send_b.at[s],
            recv_sem=recv_b.at[s], device_id=(col, s), device_id_type=MESH).wait_recv()

    for t in range(tile_count):
        term = lax.dot_general(
            tiles_ref[t], edge_out[t // per_block], (((0,), (0,)), ((), ())),
            preferred_element_type=jnp.float32)
        terms[t] = term.astype(jnp.bfloat16)

    def place(slot, carry):
        out_ref[slot] = terms[slot_tile_ref[slot]]
        return carry

    lax.fori_loop(0, out_ref.shape[0], place, 0)


def round_kernel(slot_of, slot_tile, arrived, tiles, degree, w_in, w_out, groups, per_block):
    slots, rows, channels = arrived.shape
    vmem = pl.BlockSpec(memory_space=pltpu.VMEM)
    smem = pl.BlockSpec(memory_space=pltpu.SMEM)
    return pl.pallas_call(
        functools.partial(_round_kernel, groups, per_block),
        out_shape=jax.ShapeDtypeStruct((slots, rows, channels), jnp.bfloat16),
        in_specs=[smem, smem] + [vmem] * 5,
        out_specs=vmem,
        scratch_shapes=[
            pltpu.VMEM((groups, rows, channels), jnp.float32),
            pltpu.VMEM((groups, rows, channels), jnp.float32),
            pltpu.VMEM((rows, channels), jnp.bfloat16),
            pltpu.VMEM((groups, rows, channels), jnp.bfloat16),
            pltpu.VMEM(tiles.shape, jnp.bfloat16),
            pltpu.SemaphoreType.DMA((groups,)), pltpu.SemaphoreType.DMA((groups,)),
            pltpu.SemaphoreType.DMA((groups,)), pltpu.SemaphoreType.DMA((groups,)),
        ],
        compiler_params=pltpu.CompilerParams(
            collective_id=0, has_side_effects=True, vmem_limit_bytes=48 * 1024 * 1024),
    )(slot_of, slot_tile, arrived, tiles, degree, w_in, w_out)


def _pick_kernel(asked_ref, rows_ref, out_ref, order_ref, block_ref, count_ref, sems):
    last = rows_ref.shape[0] - 1
    capacity = asked_ref.shape[2]

    def scan(slot, filled):
        block = asked_ref[slot // capacity, 0, slot % capacity]

        @pl.when(block >= 0)
        def _():
            order_ref[filled] = slot
            block_ref[filled] = jnp.minimum(block, last)

        return filled + jnp.where(block >= 0, 1, 0)

    count = lax.fori_loop(0, out_ref.shape[0], scan, 0)
    count_ref[0] = count

    def copy(i):
        return pltpu.make_async_copy(rows_ref.at[block_ref[i]], out_ref.at[order_ref[i]], sems.at[i])

    def start(i, carry):
        copy(i).start()
        return carry

    def finish(i, carry):
        copy(i).wait()
        return carry

    lax.fori_loop(0, count, start, 0)
    lax.fori_loop(0, count, finish, 0)


def pick_rows(asked, blocks):
    owners, _, capacity = asked.shape
    slots = owners * capacity
    _, rows, channels = blocks.shape
    smem = pl.BlockSpec(memory_space=pltpu.SMEM)
    return pl.pallas_call(
        _pick_kernel,
        out_shape=(
            jax.ShapeDtypeStruct((slots, rows, channels), blocks.dtype),
            jax.ShapeDtypeStruct((slots,), jnp.int32),
            jax.ShapeDtypeStruct((slots,), jnp.int32),
            jax.ShapeDtypeStruct((1,), jnp.int32),
        ),
        in_specs=[smem, pl.BlockSpec(memory_space=pltpu.VMEM)],
        out_specs=(pl.BlockSpec(memory_space=pl.ANY), smem, smem, smem),
        scratch_shapes=[pltpu.SemaphoreType.DMA((slots,))],
    )(asked, blocks)


def _land_kernel(count_ref, order_ref, block_ref, returned_ref, rows_ref, out_ref, buf, acc, sems):
    last = rows_ref.shape[0] - 1

    def copy(i):
        return pltpu.make_async_copy(returned_ref.at[order_ref[i]], buf.at[i], sems.at[i])

    def start(i, carry):
        copy(i).start()
        return carry

    lax.fori_loop(0, count_ref[0], start, 0)
    acc[...] = rows_ref[...].astype(jnp.float32)

    def add(i, carry):
        copy(i).wait()
        block = block_ref[i]
        acc[block] = acc[block] + buf[i].astype(jnp.float32)
        return carry

    lax.fori_loop(0, count_ref[0], add, 0)
    out_ref[...] = acc[...].astype(out_ref.dtype)


def land_terms(count, order, block_list, returned, blocks):
    slots, rows, channels = returned.shape
    smem = pl.BlockSpec(memory_space=pltpu.SMEM)
    return pl.pallas_call(
        _land_kernel,
        out_shape=jax.ShapeDtypeStruct(blocks.shape, blocks.dtype),
        in_specs=[smem, smem, smem, pl.BlockSpec(memory_space=pl.ANY), pl.BlockSpec(memory_space=pltpu.VMEM)],
        out_specs=pl.BlockSpec(memory_space=pltpu.VMEM),
        scratch_shapes=[
            pltpu.VMEM((slots, rows, channels), returned.dtype),
            pltpu.VMEM(blocks.shape, jnp.float32),
            pltpu.SemaphoreType.DMA((slots,)),
        ],
    )(count, order, block_list, returned, blocks)


def edge_network(summed, degrees, w_in, w_out):
    edge_in = (summed / degrees.astype(jnp.float32)[:, None]).astype(jnp.bfloat16)
    pre_act = jnp.dot(edge_in, w_in, preferred_element_type=jnp.float32)
    hidden = jax.nn.silu(pre_act).astype(jnp.bfloat16)
    return jnp.dot(hidden, w_out, preferred_element_type=jnp.float32).astype(jnp.bfloat16)


def body(node_rows, tile_values, tile_owner, tile_block, edge_degree, w_in, w_out):
    owners = lax.axis_size("wide")
    tile_count, block_size, _ = tile_values.shape
    channels = node_rows.shape[1]
    node_block_count = node_rows.shape[0] // block_size
    edge_row_count = edge_degree.shape[0]
    edge_blocks = edge_row_count // block_size
    per_block = tile_count // edge_blocks
    capacity = max(2, 2 * tile_count // owners)
    slot_count = owners * capacity
    target = tile_owner[:, 0]
    positions = jnp.arange(tile_count, dtype=jnp.int32)
    earlier = (target[:, None] == target[None, :]) & (positions[None, :] < positions[:, None])
    order_in = jnp.sum(earlier.astype(jnp.int32), axis=1)
    slot_of = target * capacity + order_in
    slot_ids = jnp.arange(slot_count, dtype=jnp.int32)
    matches = slot_of[:, None] == slot_ids[None, :]
    wanted_out = jnp.sum(jnp.where(matches, tile_block[:, None] + 1, 0), axis=0) - 1
    groups = lax.axis_size("narrow")
    me = lax.axis_index("narrow")
    own_rows = edge_row_count // groups
    own_degree = lax.dynamic_slice_in_dim(edge_degree, me * own_rows, own_rows)
    tile_of_slot = jnp.sum(jnp.where(matches, positions[:, None], 0), axis=0)
    asked = lax.all_to_all(
        wanted_out.reshape(owners, 1, capacity), "wide", split_axis=0, concat_axis=0, tiled=True
    )
    current = node_rows
    node_blocks = current.reshape(node_block_count, block_size, channels)
    degree_column = jnp.broadcast_to(own_degree.astype(jnp.float32)[:, None], (own_rows, channels))
    asked, slot_of, tile_of_slot, degree_column = lax.optimization_barrier(
        (asked, slot_of, tile_of_slot, degree_column)
    )
    picked, order, block_list, count = pick_rows(asked, node_blocks)
    arrived = lax.all_to_all(
        picked.reshape(owners, capacity, block_size, channels),
        "wide",
        split_axis=0,
        concat_axis=0,
        tiled=True,
    )
    outgoing = round_kernel(
        slot_of,
        tile_of_slot,
        arrived.reshape(slot_count, block_size, channels),
        tile_values,
        degree_column,
        w_in,
        w_out,
        groups,
        per_block,
    )
    returned = lax.all_to_all(
        outgoing.reshape(owners, capacity, block_size, channels),
        "wide",
        split_axis=0,
        concat_axis=0,
        tiled=True,
    )
    current = land_terms(
        count, order, block_list, returned.reshape(slot_count, block_size, channels), node_blocks
    ).reshape(node_block_count * block_size, channels)
    return current


def solution(mesh):
    return jax.shard_map(
        body,
        mesh=mesh,
        in_specs=(
            P(("wide", "narrow"), None),
            P(("wide", "narrow"), None, None),
            P(("wide", "narrow"), None),
            P(("wide", "narrow")),
            P("wide"),
            P(),
            P(),
        ),
        out_specs=P(("wide", "narrow"), None),
        check_vma=False,
    )
```

```python
import functools

import jax
import jax.numpy as jnp
from jax import lax
from jax.experimental import pallas as pl
from jax.experimental.pallas import tpu as pltpu
from jax.sharding import PartitionSpec as P
MESH = pl.DeviceIdType.MESH


def _round_kernel(groups, per_block, slot_of_ref, slot_tile_ref, arrived_ref, tiles_ref,
                  degree_ref, w_in_ref, w_out_ref, out_ref,
                  parts, inbox, stage, edge_out, terms, send_a, recv_a, send_b, recv_b):
    me = lax.axis_index("narrow")
    col = lax.axis_index("wide")
    tile_count = tiles_ref.shape[0]
    barrier = pltpu.get_barrier_semaphore()
    for k in range(1, groups):
        pl.semaphore_signal(barrier, inc=1, device_id=(col, lax.rem(me + k, groups)), device_id_type=MESH)

    for e in range(tile_count // per_block):
        acc = None
        for k in range(per_block):
            t = e * per_block + k
            rows = arrived_ref[slot_of_ref[t]]
            p = jnp.dot(tiles_ref[t], rows, preferred_element_type=jnp.float32)
            acc = p if acc is None else acc + p
        parts[e] = acc

    pl.semaphore_wait(barrier, groups - 1)

    def first(d):
        return pltpu.make_async_remote_copy(
            src_ref=parts.at[d], dst_ref=inbox.at[me], send_sem=send_a.at[d],
            recv_sem=recv_a.at[me], device_id=(col, d), device_id_type=MESH)

    for k in range(1, groups):
        first(lax.rem(me + k, groups)).start()
    total = parts[me]
    for k in range(1, groups):
        d = lax.rem(me + k, groups)
        s = lax.rem(me + groups - k, groups)
        first(d).wait_send()
        pltpu.make_async_remote_copy(
            src_ref=parts.at[s], dst_ref=inbox.at[s], send_sem=send_a.at[s],
            recv_sem=recv_a.at[s], device_id=(col, s), device_id_type=MESH).wait_recv()
        total = total + inbox[s]
    edge_in = (total / degree_ref[...]).astype(jnp.bfloat16)
    pre = jnp.dot(edge_in, w_in_ref[...], preferred_element_type=jnp.float32)
    hidden = (pre * jax.nn.sigmoid(pre)).astype(jnp.bfloat16)
    own = jnp.dot(hidden, w_out_ref[...], preferred_element_type=jnp.float32).astype(jnp.bfloat16)
    stage[...] = own
    edge_out[me] = own

    def second(d):
        return pltpu.make_async_remote_copy(
            src_ref=stage, dst_ref=edge_out.at[me], send_sem=send_b.at[d],
            recv_sem=recv_b.at[me], device_id=(col, d), device_id_type=MESH)

    for k in range(1, groups):
        second(lax.rem(me + k, groups)).start()

    def block_terms(e, block):
        for k in range(per_block):
            t = e * per_block + k
            term = lax.dot_general(
                tiles_ref[t], block, (((0,), (0,)), ((), ())),
                preferred_element_type=jnp.float32)
            terms[t] = term.astype(jnp.bfloat16)

    block_terms(me, own)
    for k in range(1, groups):
        d = lax.rem(me + k, groups)
        s = lax.rem(me + groups - k, groups)
        second(d).wait_send()
        pltpu.make_async_remote_copy(
            src_ref=stage, dst_ref=edge_out.at[s], send_sem=send_b.at[s],
            recv_sem=recv_b.at[s], device_id=(col, s), device_id_type=MESH).wait_recv()
        block_terms(s, edge_out[s])

    def place(slot, carry):
        out_ref[slot] = terms[slot_tile_ref[slot]]
        return carry

    lax.fori_loop(0, out_ref.shape[0], place, 0)


def round_kernel(slot_of, slot_tile, arrived, tiles, degree, w_in, w_out, groups, per_block):
    slots, rows, channels = arrived.shape
    vmem = pl.BlockSpec(memory_space=pltpu.VMEM)
    smem = pl.BlockSpec(memory_space=pltpu.SMEM)
    return pl.pallas_call(
        functools.partial(_round_kernel, groups, per_block),
        out_shape=jax.ShapeDtypeStruct((slots, rows, channels), jnp.bfloat16),
        in_specs=[smem, smem] + [vmem] * 5,
        out_specs=vmem,
        scratch_shapes=[
            pltpu.VMEM((groups, rows, channels), jnp.float32),
            pltpu.VMEM((groups, rows, channels), jnp.float32),
            pltpu.VMEM((rows, channels), jnp.bfloat16),
            pltpu.VMEM((groups, rows, channels), jnp.bfloat16),
            pltpu.VMEM(tiles.shape, jnp.bfloat16),
            pltpu.SemaphoreType.DMA((groups,)), pltpu.SemaphoreType.DMA((groups,)),
            pltpu.SemaphoreType.DMA((groups,)), pltpu.SemaphoreType.DMA((groups,)),
        ],
        compiler_params=pltpu.CompilerParams(
            collective_id=0, has_side_effects=True, vmem_limit_bytes=48 * 1024 * 1024),
    )(slot_of, slot_tile, arrived, tiles, degree, w_in, w_out)


def _pick_kernel(count_ref, order_ref, wanted_ref, rows_ref, out_ref, sems):
    last = rows_ref.shape[0] - 1

    def copy(i):
        slot = order_ref[i]
        block = jnp.clip(wanted_ref[slot], 0, last)
        return pltpu.make_async_copy(rows_ref.at[block], out_ref.at[slot], sems.at[i])

    def start(i, carry):
        copy(i).start()
        return carry

    def finish(i, carry):
        copy(i).wait()
        return carry

    lax.fori_loop(0, count_ref[0], start, 0)
    lax.fori_loop(0, count_ref[0], finish, 0)


def pick_rows(count, order, wanted, blocks):
    slots = wanted.shape[0]
    _, rows, channels = blocks.shape
    smem = pl.BlockSpec(memory_space=pltpu.SMEM)
    return pl.pallas_call(
        _pick_kernel,
        out_shape=jax.ShapeDtypeStruct((slots, rows, channels), blocks.dtype),
        in_specs=[smem, smem, smem, pl.BlockSpec(memory_space=pltpu.VMEM)],
        out_specs=pl.BlockSpec(memory_space=pl.ANY),
        scratch_shapes=[pltpu.SemaphoreType.DMA((slots,))],
    )(count, order, wanted, blocks)


def _land_kernel(count_ref, order_ref, wanted_ref, returned_ref, rows_ref, out_ref, buf, acc, sems):
    last = rows_ref.shape[0] - 1

    def copy(i):
        return pltpu.make_async_copy(returned_ref.at[order_ref[i]], buf.at[i], sems.at[i])

    def start(i, carry):
        copy(i).start()
        return carry

    lax.fori_loop(0, count_ref[0], start, 0)
    acc[...] = rows_ref[...].astype(jnp.float32)

    def add(i, carry):
        copy(i).wait()
        block = jnp.clip(wanted_ref[order_ref[i]], 0, last)
        acc[block] = acc[block] + buf[i].astype(jnp.float32)
        return carry

    lax.fori_loop(0, count_ref[0], add, 0)
    out_ref[...] = acc[...].astype(out_ref.dtype)


def land_terms(count, order, wanted, returned, blocks):
    slots, rows, channels = returned.shape
    smem = pl.BlockSpec(memory_space=pltpu.SMEM)
    return pl.pallas_call(
        _land_kernel,
        out_shape=jax.ShapeDtypeStruct(blocks.shape, blocks.dtype),
        in_specs=[smem, smem, smem, pl.BlockSpec(memory_space=pl.ANY), pl.BlockSpec(memory_space=pltpu.VMEM)],
        out_specs=pl.BlockSpec(memory_space=pltpu.VMEM),
        scratch_shapes=[
            pltpu.VMEM((slots, rows, channels), returned.dtype),
            pltpu.VMEM(blocks.shape, jnp.float32),
            pltpu.SemaphoreType.DMA((slots,)),
        ],
    )(count, order, wanted, returned, blocks)


def edge_network(summed, degrees, w_in, w_out):
    edge_in = (summed / degrees.astype(jnp.float32)[:, None]).astype(jnp.bfloat16)
    pre_act = jnp.dot(edge_in, w_in, preferred_element_type=jnp.float32)
    hidden = jax.nn.silu(pre_act).astype(jnp.bfloat16)
    return jnp.dot(hidden, w_out, preferred_element_type=jnp.float32).astype(jnp.bfloat16)


def body(node_rows, tile_values, tile_owner, tile_block, edge_degree, w_in, w_out):
    owners = lax.axis_size("wide")
    tile_count, block_size, _ = tile_values.shape
    channels = node_rows.shape[1]
    node_block_count = node_rows.shape[0] // block_size
    edge_row_count = edge_degree.shape[0]
    edge_blocks = edge_row_count // block_size
    per_block = tile_count // edge_blocks
    capacity = max(2, 2 * tile_count // owners)
    slot_count = owners * capacity
    target = tile_owner[:, 0]
    positions = jnp.arange(tile_count, dtype=jnp.int32)
    earlier = (target[:, None] == target[None, :]) & (positions[None, :] < positions[:, None])
    order_in = jnp.sum(earlier.astype(jnp.int32), axis=1)
    slot_of = target * capacity + order_in
    slot_ids = jnp.arange(slot_count, dtype=jnp.int32)
    matches = slot_of[:, None] == slot_ids[None, :]
    wanted_out = jnp.sum(jnp.where(matches, tile_block[:, None] + 1, 0), axis=0) - 1
    groups = lax.axis_size("narrow")
    me = lax.axis_index("narrow")
    own_rows = edge_row_count // groups
    own_degree = lax.dynamic_slice_in_dim(edge_degree, me * own_rows, own_rows)
    tile_of_slot = jnp.sum(jnp.where(matches, positions[:, None], 0), axis=0)
    wanted = lax.all_to_all(
        wanted_out.reshape(owners, capacity), "wide", split_axis=0, concat_axis=0, tiled=True
    ).reshape(slot_count)
    current = node_rows
    node_blocks = current.reshape(node_block_count, block_size, channels)
    degree_column = jnp.broadcast_to(own_degree.astype(jnp.float32)[:, None], (own_rows, channels))
    wanted, slot_of, tile_of_slot, degree_column = lax.optimization_barrier(
        (wanted, slot_of, tile_of_slot, degree_column)
    )
    filled = wanted >= 0
    rank = jnp.cumsum(filled.astype(jnp.int32)) - 1
    count = jnp.sum(filled.astype(jnp.int32)).reshape(1)
    order = jnp.sum(
        jnp.where(filled[None, :] & (rank[None, :] == slot_ids[:, None]), slot_ids[None, :], 0),
        axis=1,
    )
    picked = pick_rows(count, order, wanted, node_blocks)
    arrived = lax.all_to_all(
        picked.reshape(owners, capacity, block_size, channels),
        "wide",
        split_axis=0,
        concat_axis=0,
        tiled=True,
    )
    outgoing = round_kernel(
        slot_of,
        tile_of_slot,
        arrived.reshape(slot_count, block_size, channels),
        tile_values,
        degree_column,
        w_in,
        w_out,
        groups,
        per_block,
    )
    returned = lax.all_to_all(
        outgoing.reshape(owners, capacity, block_size, channels),
        "wide",
        split_axis=0,
        concat_axis=0,
        tiled=True,
    )
    current = land_terms(
        count, order, wanted, returned.reshape(slot_count, block_size, channels), node_blocks
    ).reshape(node_block_count * block_size, channels)
    return current


def solution(mesh):
    return jax.shard_map(
        body,
        mesh=mesh,
        in_specs=(
            P(("wide", "narrow"), None),
            P(("wide", "narrow"), None, None),
            P(("wide", "narrow"), None),
            P(("wide", "narrow")),
            P("wide"),
            P(),
            P(),
        ),
        out_specs=P(("wide", "narrow"), None),
        check_vma=False,
    )
```

```python
import functools

import jax
import jax.numpy as jnp
from jax import lax
from jax.experimental import pallas as pl
from jax.experimental.pallas import tpu as pltpu
from jax.sharding import PartitionSpec as P
MESH = pl.DeviceIdType.MESH


def _round_kernel(groups, per_block, slot_of_ref, slot_tile_ref, arrived_ref, tiles_ref,
                  degree_ref, w_in_ref, w_out_ref, out_ref,
                  parts, inbox, stage, edge_out, terms, send_a, recv_a, send_b, recv_b, exact):
    me = lax.axis_index("narrow")
    col = lax.axis_index("wide")
    tile_count = tiles_ref.shape[0]
    barrier = pltpu.get_barrier_semaphore()
    for k in range(1, groups):
        pl.semaphore_signal(barrier, inc=1, device_id=(col, lax.rem(me + k, groups)), device_id_type=MESH)

    for e in range(tile_count // per_block):
        acc = None
        for k in range(per_block):
            t = e * per_block + k
            rows = arrived_ref[slot_of_ref[t]]
            p = jnp.dot(tiles_ref[t], rows, preferred_element_type=jnp.float32)
            acc = p if acc is None else acc + p
        parts[e] = acc.astype(parts.dtype)
        exact[e] = acc

    pl.semaphore_wait(barrier, groups - 1)

    def first(d):
        return pltpu.make_async_remote_copy(
            src_ref=parts.at[d], dst_ref=inbox.at[me], send_sem=send_a.at[d],
            recv_sem=recv_a.at[me], device_id=(col, d), device_id_type=MESH)

    for k in range(1, groups):
        first(lax.rem(me + k, groups)).start()
    total = exact[me]
    for k in range(1, groups):
        d = lax.rem(me + k, groups)
        s = lax.rem(me + groups - k, groups)
        first(d).wait_send()
        pltpu.make_async_remote_copy(
            src_ref=parts.at[s], dst_ref=inbox.at[s], send_sem=send_a.at[s],
            recv_sem=recv_a.at[s], device_id=(col, s), device_id_type=MESH).wait_recv()
        total = total + inbox[s].astype(jnp.float32)
    edge_in = (total / degree_ref[...]).astype(jnp.bfloat16)
    pre = jnp.dot(edge_in, w_in_ref[...], preferred_element_type=jnp.float32)
    hidden = (pre * jax.nn.sigmoid(pre)).astype(jnp.bfloat16)
    own = jnp.dot(hidden, w_out_ref[...], preferred_element_type=jnp.float32).astype(jnp.bfloat16)
    stage[...] = own
    edge_out[me] = own

    def second(d):
        return pltpu.make_async_remote_copy(
            src_ref=stage, dst_ref=edge_out.at[me], send_sem=send_b.at[d],
            recv_sem=recv_b.at[me], device_id=(col, d), device_id_type=MESH)

    for k in range(1, groups):
        second(lax.rem(me + k, groups)).start()

    def block_terms(e, block):
        for k in range(per_block):
            t = e * per_block + k
            term = lax.dot_general(
                tiles_ref[t], block, (((0,), (0,)), ((), ())),
                preferred_element_type=jnp.float32)
            terms[t] = term.astype(jnp.bfloat16)

    block_terms(me, own)
    for k in range(1, groups):
        d = lax.rem(me + k, groups)
        s = lax.rem(me + groups - k, groups)
        second(d).wait_send()
        pltpu.make_async_remote_copy(
            src_ref=stage, dst_ref=edge_out.at[s], send_sem=send_b.at[s],
            recv_sem=recv_b.at[s], device_id=(col, s), device_id_type=MESH).wait_recv()
        block_terms(s, edge_out[s])

    def place(slot, carry):
        out_ref[slot] = terms[slot_tile_ref[slot]]
        return carry

    lax.fori_loop(0, out_ref.shape[0], place, 0)


def round_kernel(slot_of, slot_tile, arrived, tiles, degree, w_in, w_out, groups, per_block):
    slots, rows, channels = arrived.shape
    vmem = pl.BlockSpec(memory_space=pltpu.VMEM)
    smem = pl.BlockSpec(memory_space=pltpu.SMEM)
    return pl.pallas_call(
        functools.partial(_round_kernel, groups, per_block),
        out_shape=jax.ShapeDtypeStruct((slots, rows, channels), jnp.bfloat16),
        in_specs=[smem, smem] + [vmem] * 5,
        out_specs=vmem,
        scratch_shapes=[
            pltpu.VMEM((groups, rows, channels), jnp.bfloat16),
            pltpu.VMEM((groups, rows, channels), jnp.bfloat16),
            pltpu.VMEM((rows, channels), jnp.bfloat16),
            pltpu.VMEM((groups, rows, channels), jnp.bfloat16),
            pltpu.VMEM(tiles.shape, jnp.bfloat16),
            pltpu.SemaphoreType.DMA((groups,)), pltpu.SemaphoreType.DMA((groups,)),
            pltpu.SemaphoreType.DMA((groups,)), pltpu.SemaphoreType.DMA((groups,)),
            pltpu.VMEM((groups, rows, channels), jnp.float32),
        ],
        compiler_params=pltpu.CompilerParams(
            collective_id=0, has_side_effects=True, vmem_limit_bytes=48 * 1024 * 1024),
    )(slot_of, slot_tile, arrived, tiles, degree, w_in, w_out)


def _pick_kernel(count_ref, order_ref, wanted_ref, rows_ref, out_ref, sems):
    last = rows_ref.shape[0] - 1

    def copy(i):
        slot = order_ref[i]
        block = jnp.clip(wanted_ref[slot], 0, last)
        return pltpu.make_async_copy(rows_ref.at[block], out_ref.at[slot], sems.at[i])

    def start(i, carry):
        copy(i).start()
        return carry

    def finish(i, carry):
        copy(i).wait()
        return carry

    lax.fori_loop(0, count_ref[0], start, 0)
    lax.fori_loop(0, count_ref[0], finish, 0)


def pick_rows(count, order, wanted, blocks):
    slots = wanted.shape[0]
    _, rows, channels = blocks.shape
    smem = pl.BlockSpec(memory_space=pltpu.SMEM)
    return pl.pallas_call(
        _pick_kernel,
        out_shape=jax.ShapeDtypeStruct((slots, rows, channels), blocks.dtype),
        in_specs=[smem, smem, smem, pl.BlockSpec(memory_space=pltpu.VMEM)],
        out_specs=pl.BlockSpec(memory_space=pl.ANY),
        scratch_shapes=[pltpu.SemaphoreType.DMA((slots,))],
    )(count, order, wanted, blocks)


def _land_kernel(count_ref, order_ref, wanted_ref, returned_ref, rows_ref, out_ref, buf, acc, sems):
    last = rows_ref.shape[0] - 1

    def copy(i):
        return pltpu.make_async_copy(returned_ref.at[order_ref[i]], buf.at[i], sems.at[i])

    def start(i, carry):
        copy(i).start()
        return carry

    lax.fori_loop(0, count_ref[0], start, 0)
    acc[...] = rows_ref[...].astype(jnp.float32)

    def add(i, carry):
        copy(i).wait()
        block = jnp.clip(wanted_ref[order_ref[i]], 0, last)
        acc[block] = acc[block] + buf[i].astype(jnp.float32)
        return carry

    lax.fori_loop(0, count_ref[0], add, 0)
    out_ref[...] = acc[...].astype(out_ref.dtype)


def land_terms(count, order, wanted, returned, blocks):
    slots, rows, channels = returned.shape
    smem = pl.BlockSpec(memory_space=pltpu.SMEM)
    return pl.pallas_call(
        _land_kernel,
        out_shape=jax.ShapeDtypeStruct(blocks.shape, blocks.dtype),
        in_specs=[smem, smem, smem, pl.BlockSpec(memory_space=pl.ANY), pl.BlockSpec(memory_space=pltpu.VMEM)],
        out_specs=pl.BlockSpec(memory_space=pltpu.VMEM),
        scratch_shapes=[
            pltpu.VMEM((slots, rows, channels), returned.dtype),
            pltpu.VMEM(blocks.shape, jnp.float32),
            pltpu.SemaphoreType.DMA((slots,)),
        ],
    )(count, order, wanted, returned, blocks)


def edge_network(summed, degrees, w_in, w_out):
    edge_in = (summed / degrees.astype(jnp.float32)[:, None]).astype(jnp.bfloat16)
    pre_act = jnp.dot(edge_in, w_in, preferred_element_type=jnp.float32)
    hidden = jax.nn.silu(pre_act).astype(jnp.bfloat16)
    return jnp.dot(hidden, w_out, preferred_element_type=jnp.float32).astype(jnp.bfloat16)


def body(node_rows, tile_values, tile_owner, tile_block, edge_degree, w_in, w_out):
    owners = lax.axis_size("wide")
    tile_count, block_size, _ = tile_values.shape
    channels = node_rows.shape[1]
    node_block_count = node_rows.shape[0] // block_size
    edge_row_count = edge_degree.shape[0]
    edge_blocks = edge_row_count // block_size
    per_block = tile_count // edge_blocks
    capacity = max(2, 2 * tile_count // owners)
    slot_count = owners * capacity
    target = tile_owner[:, 0]
    positions = jnp.arange(tile_count, dtype=jnp.int32)
    earlier = (target[:, None] == target[None, :]) & (positions[None, :] < positions[:, None])
    order_in = jnp.sum(earlier.astype(jnp.int32), axis=1)
    slot_of = target * capacity + order_in
    slot_ids = jnp.arange(slot_count, dtype=jnp.int32)
    matches = slot_of[:, None] == slot_ids[None, :]
    wanted_out = jnp.sum(jnp.where(matches, tile_block[:, None] + 1, 0), axis=0) - 1
    groups = lax.axis_size("narrow")
    me = lax.axis_index("narrow")
    own_rows = edge_row_count // groups
    own_degree = lax.dynamic_slice_in_dim(edge_degree, me * own_rows, own_rows)
    tile_of_slot = jnp.sum(jnp.where(matches, positions[:, None], 0), axis=0)
    wanted = lax.all_to_all(
        wanted_out.reshape(owners, capacity), "wide", split_axis=0, concat_axis=0, tiled=True
    ).reshape(slot_count)
    current = node_rows
    node_blocks = current.reshape(node_block_count, block_size, channels)
    degree_column = jnp.broadcast_to(own_degree.astype(jnp.float32)[:, None], (own_rows, channels))
    wanted, slot_of, tile_of_slot, degree_column = lax.optimization_barrier(
        (wanted, slot_of, tile_of_slot, degree_column)
    )
    filled = wanted >= 0
    rank = jnp.cumsum(filled.astype(jnp.int32)) - 1
    count = jnp.sum(filled.astype(jnp.int32)).reshape(1)
    order = jnp.sum(
        jnp.where(filled[None, :] & (rank[None, :] == slot_ids[:, None]), slot_ids[None, :], 0),
        axis=1,
    )
    picked = pick_rows(count, order, wanted, node_blocks)
    arrived = lax.all_to_all(
        picked.reshape(owners, capacity, block_size, channels),
        "wide",
        split_axis=0,
        concat_axis=0,
        tiled=True,
    )
    outgoing = round_kernel(
        slot_of,
        tile_of_slot,
        arrived.reshape(slot_count, block_size, channels),
        tile_values,
        degree_column,
        w_in,
        w_out,
        groups,
        per_block,
    )
    returned = lax.all_to_all(
        outgoing.reshape(owners, capacity, block_size, channels),
        "wide",
        split_axis=0,
        concat_axis=0,
        tiled=True,
    )
    current = land_terms(
        count, order, wanted, returned.reshape(slot_count, block_size, channels), node_blocks
    ).reshape(node_block_count * block_size, channels)
    return current


def solution(mesh):
    return jax.shard_map(
        body,
        mesh=mesh,
        in_specs=(
            P(("wide", "narrow"), None),
            P(("wide", "narrow"), None, None),
            P(("wide", "narrow"), None),
            P(("wide", "narrow")),
            P("wide"),
            P(),
            P(),
        ),
        out_specs=P(("wide", "narrow"), None),
        check_vma=False,
    )
```

```python
import functools

import jax
import jax.numpy as jnp
from jax import lax
from jax.experimental import pallas as pl
from jax.experimental.pallas import tpu as pltpu
from jax.sharding import PartitionSpec as P
MESH = pl.DeviceIdType.MESH


def _round_kernel(groups, per_block, slot_of_ref, slot_tile_ref, arrived_ref, tiles_ref,
                  degree_ref, w_in_ref, w_out_ref, out_ref,
                  parts, inbox, stage, edge_out, terms, send_a, recv_a, send_b, recv_b):
    me = lax.axis_index("narrow")
    col = lax.axis_index("wide")
    tile_count = tiles_ref.shape[0]
    barrier = pltpu.get_barrier_semaphore()
    for k in range(1, groups):
        pl.semaphore_signal(barrier, inc=1, device_id=(col, lax.rem(me + k, groups)), device_id_type=MESH)

    for e in range(tile_count // per_block):
        acc = None
        for k in range(per_block):
            t = e * per_block + k
            rows = arrived_ref[slot_of_ref[t]]
            p = jnp.dot(tiles_ref[t], rows, preferred_element_type=jnp.float32)
            acc = p if acc is None else acc + p
        parts[e] = acc

    pl.semaphore_wait(barrier, groups - 1)

    def first(d):
        return pltpu.make_async_remote_copy(
            src_ref=parts.at[d], dst_ref=inbox.at[me], send_sem=send_a.at[d],
            recv_sem=recv_a.at[me], device_id=(col, d), device_id_type=MESH)

    for k in range(1, groups):
        first(lax.rem(me + k, groups)).start()
    total = parts[me]
    for k in range(1, groups):
        d = lax.rem(me + k, groups)
        s = lax.rem(me + groups - k, groups)
        first(d).wait_send()
        pltpu.make_async_remote_copy(
            src_ref=parts.at[s], dst_ref=inbox.at[s], send_sem=send_a.at[s],
            recv_sem=recv_a.at[s], device_id=(col, s), device_id_type=MESH).wait_recv()
        total = total + inbox[s]
    edge_in = (total / degree_ref[...]).astype(jnp.bfloat16)
    pre = jnp.dot(edge_in, w_in_ref[...], preferred_element_type=jnp.float32)
    hidden = (pre * jax.nn.sigmoid(pre)).astype(jnp.bfloat16)
    own = jnp.dot(hidden, w_out_ref[...], preferred_element_type=jnp.float32).astype(jnp.bfloat16)
    stage[...] = own
    edge_out[me] = own

    def second(d):
        return pltpu.make_async_remote_copy(
            src_ref=stage, dst_ref=edge_out.at[me], send_sem=send_b.at[d],
            recv_sem=recv_b.at[me], device_id=(col, d), device_id_type=MESH)

    for k in range(1, groups):
        second(lax.rem(me + k, groups)).start()

    def block_terms(e, block):
        for k in range(per_block):
            t = e * per_block + k
            term = lax.dot_general(
                tiles_ref[t], block, (((0,), (0,)), ((), ())),
                preferred_element_type=jnp.float32)
            terms[t] = term.astype(jnp.bfloat16)

    block_terms(me, own)
    for k in range(1, groups):
        d = lax.rem(me + k, groups)
        s = lax.rem(me + groups - k, groups)
        second(d).wait_send()
        pltpu.make_async_remote_copy(
            src_ref=stage, dst_ref=edge_out.at[s], send_sem=send_b.at[s],
            recv_sem=recv_b.at[s], device_id=(col, s), device_id_type=MESH).wait_recv()
        block_terms(s, edge_out[s])

    def place(slot, carry):
        out_ref[slot] = terms[slot_tile_ref[slot]]
        return carry

    lax.fori_loop(0, out_ref.shape[0], place, 0, unroll=8)


def round_kernel(slot_of, slot_tile, arrived, tiles, degree, w_in, w_out, groups, per_block):
    slots, rows, channels = arrived.shape
    vmem = pl.BlockSpec(memory_space=pltpu.VMEM)
    smem = pl.BlockSpec(memory_space=pltpu.SMEM)
    return pl.pallas_call(
        functools.partial(_round_kernel, groups, per_block),
        out_shape=jax.ShapeDtypeStruct((slots, rows, channels), jnp.bfloat16),
        in_specs=[smem, smem] + [vmem] * 5,
        out_specs=vmem,
        scratch_shapes=[
            pltpu.VMEM((groups, rows, channels), jnp.float32),
            pltpu.VMEM((groups, rows, channels), jnp.float32),
            pltpu.VMEM((rows, channels), jnp.bfloat16),
            pltpu.VMEM((groups, rows, channels), jnp.bfloat16),
            pltpu.VMEM(tiles.shape, jnp.bfloat16),
            pltpu.SemaphoreType.DMA((groups,)), pltpu.SemaphoreType.DMA((groups,)),
            pltpu.SemaphoreType.DMA((groups,)), pltpu.SemaphoreType.DMA((groups,)),
        ],
        compiler_params=pltpu.CompilerParams(
            collective_id=0, has_side_effects=True, vmem_limit_bytes=48 * 1024 * 1024),
    )(slot_of, slot_tile, arrived, tiles, degree, w_in, w_out)


def _pick_kernel(count_ref, order_ref, wanted_ref, rows_ref, out_ref, sems):
    last = rows_ref.shape[0] - 1

    def copy(i):
        slot = order_ref[i]
        block = jnp.clip(wanted_ref[slot], 0, last)
        return pltpu.make_async_copy(rows_ref.at[block], out_ref.at[slot], sems.at[i])

    def start(i, carry):
        copy(i).start()
        return carry

    def finish(i, carry):
        copy(i).wait()
        return carry

    lax.fori_loop(0, count_ref[0], start, 0)
    lax.fori_loop(0, count_ref[0], finish, 0)


def pick_rows(count, order, wanted, blocks):
    slots = wanted.shape[0]
    _, rows, channels = blocks.shape
    smem = pl.BlockSpec(memory_space=pltpu.SMEM)
    return pl.pallas_call(
        _pick_kernel,
        out_shape=jax.ShapeDtypeStruct((slots, rows, channels), blocks.dtype),
        in_specs=[smem, smem, smem, pl.BlockSpec(memory_space=pltpu.VMEM)],
        out_specs=pl.BlockSpec(memory_space=pl.ANY),
        scratch_shapes=[pltpu.SemaphoreType.DMA((slots,))],
    )(count, order, wanted, blocks)


def _land_kernel(count_ref, order_ref, wanted_ref, returned_ref, rows_ref, out_ref, buf, acc, sems):
    last = rows_ref.shape[0] - 1

    def copy(i):
        return pltpu.make_async_copy(returned_ref.at[order_ref[i]], buf.at[i], sems.at[i])

    def start(i, carry):
        copy(i).start()
        return carry

    lax.fori_loop(0, count_ref[0], start, 0)
    acc[...] = rows_ref[...].astype(jnp.float32)

    def add(i, carry):
        copy(i).wait()
        block = jnp.clip(wanted_ref[order_ref[i]], 0, last)
        acc[block] = acc[block] + buf[i].astype(jnp.float32)
        return carry

    lax.fori_loop(0, count_ref[0], add, 0)
    out_ref[...] = acc[...].astype(out_ref.dtype)


def land_terms(count, order, wanted, returned, blocks):
    slots, rows, channels = returned.shape
    smem = pl.BlockSpec(memory_space=pltpu.SMEM)
    return pl.pallas_call(
        _land_kernel,
        out_shape=jax.ShapeDtypeStruct(blocks.shape, blocks.dtype),
        in_specs=[smem, smem, smem, pl.BlockSpec(memory_space=pl.ANY), pl.BlockSpec(memory_space=pltpu.VMEM)],
        out_specs=pl.BlockSpec(memory_space=pltpu.VMEM),
        scratch_shapes=[
            pltpu.VMEM((slots, rows, channels), returned.dtype),
            pltpu.VMEM(blocks.shape, jnp.float32),
            pltpu.SemaphoreType.DMA((slots,)),
        ],
    )(count, order, wanted, returned, blocks)


def edge_network(summed, degrees, w_in, w_out):
    edge_in = (summed / degrees.astype(jnp.float32)[:, None]).astype(jnp.bfloat16)
    pre_act = jnp.dot(edge_in, w_in, preferred_element_type=jnp.float32)
    hidden = jax.nn.silu(pre_act).astype(jnp.bfloat16)
    return jnp.dot(hidden, w_out, preferred_element_type=jnp.float32).astype(jnp.bfloat16)


def body(node_rows, tile_values, tile_owner, tile_block, edge_degree, w_in, w_out):
    owners = lax.axis_size("wide")
    tile_count, block_size, _ = tile_values.shape
    channels = node_rows.shape[1]
    node_block_count = node_rows.shape[0] // block_size
    edge_row_count = edge_degree.shape[0]
    edge_blocks = edge_row_count // block_size
    per_block = tile_count // edge_blocks
    capacity = max(2, 2 * tile_count // owners)
    slot_count = owners * capacity
    target = tile_owner[:, 0]
    positions = jnp.arange(tile_count, dtype=jnp.int32)
    earlier = (target[:, None] == target[None, :]) & (positions[None, :] < positions[:, None])
    order_in = jnp.sum(earlier.astype(jnp.int32), axis=1)
    slot_of = target * capacity + order_in
    slot_ids = jnp.arange(slot_count, dtype=jnp.int32)
    matches = slot_of[:, None] == slot_ids[None, :]
    wanted_out = jnp.sum(jnp.where(matches, tile_block[:, None] + 1, 0), axis=0) - 1
    groups = lax.axis_size("narrow")
    me = lax.axis_index("narrow")
    own_rows = edge_row_count // groups
    own_degree = lax.dynamic_slice_in_dim(edge_degree, me * own_rows, own_rows)
    tile_of_slot = jnp.sum(jnp.where(matches, positions[:, None], 0), axis=0)
    wanted = lax.all_to_all(
        wanted_out.reshape(owners, capacity), "wide", split_axis=0, concat_axis=0, tiled=True
    ).reshape(slot_count)
    current = node_rows
    node_blocks = current.reshape(node_block_count, block_size, channels)
    degree_column = jnp.broadcast_to(own_degree.astype(jnp.float32)[:, None], (own_rows, channels))
    wanted, slot_of, tile_of_slot, degree_column = lax.optimization_barrier(
        (wanted, slot_of, tile_of_slot, degree_column)
    )
    filled = wanted >= 0
    rank = jnp.cumsum(filled.astype(jnp.int32)) - 1
    count = jnp.sum(filled.astype(jnp.int32)).reshape(1)
    order = jnp.sum(
        jnp.where(filled[None, :] & (rank[None, :] == slot_ids[:, None]), slot_ids[None, :], 0),
        axis=1,
    )
    picked = pick_rows(count, order, wanted, node_blocks)
    arrived = lax.all_to_all(
        picked.reshape(owners, capacity, block_size, channels),
        "wide",
        split_axis=0,
        concat_axis=0,
        tiled=True,
    )
    outgoing = round_kernel(
        slot_of,
        tile_of_slot,
        arrived.reshape(slot_count, block_size, channels),
        tile_values,
        degree_column,
        w_in,
        w_out,
        groups,
        per_block,
    )
    returned = lax.all_to_all(
        outgoing.reshape(owners, capacity, block_size, channels),
        "wide",
        split_axis=0,
        concat_axis=0,
        tiled=True,
    )
    current = land_terms(
        count, order, wanted, returned.reshape(slot_count, block_size, channels), node_blocks
    ).reshape(node_block_count * block_size, channels)
    return current


def solution(mesh):
    return jax.shard_map(
        body,
        mesh=mesh,
        in_specs=(
            P(("wide", "narrow"), None),
            P(("wide", "narrow"), None, None),
            P(("wide", "narrow"), None),
            P(("wide", "narrow")),
            P("wide"),
            P(),
            P(),
        ),
        out_specs=P(("wide", "narrow"), None),
        check_vma=False,
    )
```

```python
import functools

import jax
import jax.numpy as jnp
from jax import lax
from jax.experimental import pallas as pl
from jax.experimental.pallas import tpu as pltpu
from jax.sharding import PartitionSpec as P
MESH = pl.DeviceIdType.MESH


def _round_kernel(groups, per_block, slot_tile_ref, parts, tiles_ref,
                  degree_ref, w_in_ref, w_out_ref, out_ref,
                  inbox, stage, edge_out, terms, send_a, recv_a, send_b, recv_b):
    me = lax.axis_index("narrow")
    col = lax.axis_index("wide")
    tile_count = tiles_ref.shape[0]
    barrier = pltpu.get_barrier_semaphore()
    for k in range(1, groups):
        pl.semaphore_signal(barrier, inc=1, device_id=(col, lax.rem(me + k, groups)), device_id_type=MESH)

    pl.semaphore_wait(barrier, groups - 1)

    def first(d):
        return pltpu.make_async_remote_copy(
            src_ref=parts.at[d], dst_ref=inbox.at[me], send_sem=send_a.at[d],
            recv_sem=recv_a.at[me], device_id=(col, d), device_id_type=MESH)

    for k in range(1, groups):
        first(lax.rem(me + k, groups)).start()
    total = parts[me]
    for k in range(1, groups):
        d = lax.rem(me + k, groups)
        s = lax.rem(me + groups - k, groups)
        first(d).wait_send()
        pltpu.make_async_remote_copy(
            src_ref=parts.at[s], dst_ref=inbox.at[s], send_sem=send_a.at[s],
            recv_sem=recv_a.at[s], device_id=(col, s), device_id_type=MESH).wait_recv()
        total = total + inbox[s]
    edge_in = (total / degree_ref[...]).astype(jnp.bfloat16)
    pre = jnp.dot(edge_in, w_in_ref[...], preferred_element_type=jnp.float32)
    hidden = (pre * jax.nn.sigmoid(pre)).astype(jnp.bfloat16)
    own = jnp.dot(hidden, w_out_ref[...], preferred_element_type=jnp.float32).astype(jnp.bfloat16)
    stage[...] = own
    edge_out[me] = own

    def second(d):
        return pltpu.make_async_remote_copy(
            src_ref=stage, dst_ref=edge_out.at[me], send_sem=send_b.at[d],
            recv_sem=recv_b.at[me], device_id=(col, d), device_id_type=MESH)

    for k in range(1, groups):
        second(lax.rem(me + k, groups)).start()

    def block_terms(e, block):
        for k in range(per_block):
            t = e * per_block + k
            term = lax.dot_general(
                tiles_ref[t], block, (((0,), (0,)), ((), ())),
                preferred_element_type=jnp.float32)
            terms[t] = term.astype(jnp.bfloat16)

    block_terms(me, own)
    for k in range(1, groups):
        d = lax.rem(me + k, groups)
        s = lax.rem(me + groups - k, groups)
        second(d).wait_send()
        pltpu.make_async_remote_copy(
            src_ref=stage, dst_ref=edge_out.at[s], send_sem=send_b.at[s],
            recv_sem=recv_b.at[s], device_id=(col, s), device_id_type=MESH).wait_recv()
        block_terms(s, edge_out[s])

    def place(slot, carry):
        out_ref[slot] = terms[slot_tile_ref[slot]]
        return carry

    lax.fori_loop(0, out_ref.shape[0], place, 0, unroll=8)


def _product_kernel(per_block, slot_of_ref, arrived_ref, tiles_ref, out_ref, rows, sems):
    last = arrived_ref.shape[0] - 1
    copies = [
        pltpu.make_async_copy(
            arrived_ref.at[jnp.minimum(slot_of_ref[t], last)], rows.at[t], sems.at[t])
        for t in range(tiles_ref.shape[0])
    ]
    for copy in copies:
        copy.start()
    for e in range(out_ref.shape[0]):
        acc = None
        for k in range(per_block):
            t = e * per_block + k
            copies[t].wait()
            p = jnp.dot(tiles_ref[t], rows[t], preferred_element_type=jnp.float32)
            acc = p if acc is None else acc + p
        out_ref[e] = acc


def tile_products(slot_of, arrived, tiles, per_block):
    count, rows, channels = tiles.shape
    return pl.pallas_call(
        functools.partial(_product_kernel, per_block),
        out_shape=jax.ShapeDtypeStruct((count // per_block, rows, channels), jnp.float32),
        in_specs=[
            pl.BlockSpec(memory_space=pltpu.SMEM),
            pl.BlockSpec(memory_space=pl.ANY),
            pl.BlockSpec(memory_space=pltpu.VMEM),
        ],
        out_specs=pl.BlockSpec(memory_space=pltpu.VMEM),
        scratch_shapes=[pltpu.VMEM(tiles.shape, tiles.dtype), pltpu.SemaphoreType.DMA((count,))],
    )(slot_of, arrived, tiles)


def round_kernel(slot_tile, parts, slots, tiles, degree, w_in, w_out, groups, per_block):
    _, rows, channels = parts.shape
    vmem = pl.BlockSpec(memory_space=pltpu.VMEM)
    smem = pl.BlockSpec(memory_space=pltpu.SMEM)
    return pl.pallas_call(
        functools.partial(_round_kernel, groups, per_block),
        out_shape=jax.ShapeDtypeStruct((slots, rows, channels), jnp.bfloat16),
        in_specs=[smem] + [vmem] * 5,
        out_specs=vmem,
        scratch_shapes=[
            pltpu.VMEM((groups, rows, channels), jnp.float32),
            pltpu.VMEM((rows, channels), jnp.bfloat16),
            pltpu.VMEM((groups, rows, channels), jnp.bfloat16),
            pltpu.VMEM(tiles.shape, jnp.bfloat16),
            pltpu.SemaphoreType.DMA((groups,)), pltpu.SemaphoreType.DMA((groups,)),
            pltpu.SemaphoreType.DMA((groups,)), pltpu.SemaphoreType.DMA((groups,)),
        ],
        compiler_params=pltpu.CompilerParams(
            collective_id=0, has_side_effects=True, vmem_limit_bytes=48 * 1024 * 1024),
    )(slot_tile, parts, tiles, degree, w_in, w_out)


def _pick_kernel(count_ref, order_ref, wanted_ref, rows_ref, out_ref, sems):
    last = rows_ref.shape[0] - 1

    def copy(i):
        slot = order_ref[i]
        block = jnp.clip(wanted_ref[slot], 0, last)
        return pltpu.make_async_copy(rows_ref.at[block], out_ref.at[slot], sems.at[i])

    def start(i, carry):
        copy(i).start()
        return carry

    def finish(i, carry):
        copy(i).wait()
        return carry

    lax.fori_loop(0, count_ref[0], start, 0)
    lax.fori_loop(0, count_ref[0], finish, 0)


def pick_rows(count, order, wanted, blocks):
    slots = wanted.shape[0]
    _, rows, channels = blocks.shape
    smem = pl.BlockSpec(memory_space=pltpu.SMEM)
    return pl.pallas_call(
        _pick_kernel,
        out_shape=jax.ShapeDtypeStruct((slots, rows, channels), blocks.dtype),
        in_specs=[smem, smem, smem, pl.BlockSpec(memory_space=pltpu.VMEM)],
        out_specs=pl.BlockSpec(memory_space=pl.ANY),
        scratch_shapes=[pltpu.SemaphoreType.DMA((slots,))],
    )(count, order, wanted, blocks)


def _land_kernel(count_ref, order_ref, wanted_ref, returned_ref, rows_ref, out_ref, buf, acc, sems):
    last = rows_ref.shape[0] - 1

    def copy(i):
        return pltpu.make_async_copy(returned_ref.at[order_ref[i]], buf.at[i], sems.at[i])

    def start(i, carry):
        copy(i).start()
        return carry

    lax.fori_loop(0, count_ref[0], start, 0)
    acc[...] = rows_ref[...].astype(jnp.float32)

    def add(i, carry):
        copy(i).wait()
        block = jnp.clip(wanted_ref[order_ref[i]], 0, last)
        acc[block] = acc[block] + buf[i].astype(jnp.float32)
        return carry

    lax.fori_loop(0, count_ref[0], add, 0)
    out_ref[...] = acc[...].astype(out_ref.dtype)


def land_terms(count, order, wanted, returned, blocks):
    slots, rows, channels = returned.shape
    smem = pl.BlockSpec(memory_space=pltpu.SMEM)
    return pl.pallas_call(
        _land_kernel,
        out_shape=jax.ShapeDtypeStruct(blocks.shape, blocks.dtype),
        in_specs=[smem, smem, smem, pl.BlockSpec(memory_space=pl.ANY), pl.BlockSpec(memory_space=pltpu.VMEM)],
        out_specs=pl.BlockSpec(memory_space=pltpu.VMEM),
        scratch_shapes=[
            pltpu.VMEM((slots, rows, channels), returned.dtype),
            pltpu.VMEM(blocks.shape, jnp.float32),
            pltpu.SemaphoreType.DMA((slots,)),
        ],
    )(count, order, wanted, returned, blocks)


def edge_network(summed, degrees, w_in, w_out):
    edge_in = (summed / degrees.astype(jnp.float32)[:, None]).astype(jnp.bfloat16)
    pre_act = jnp.dot(edge_in, w_in, preferred_element_type=jnp.float32)
    hidden = jax.nn.silu(pre_act).astype(jnp.bfloat16)
    return jnp.dot(hidden, w_out, preferred_element_type=jnp.float32).astype(jnp.bfloat16)


def body(node_rows, tile_values, tile_owner, tile_block, edge_degree, w_in, w_out):
    owners = lax.axis_size("wide")
    tile_count, block_size, _ = tile_values.shape
    channels = node_rows.shape[1]
    node_block_count = node_rows.shape[0] // block_size
    edge_row_count = edge_degree.shape[0]
    edge_blocks = edge_row_count // block_size
    per_block = tile_count // edge_blocks
    capacity = max(2, 2 * tile_count // owners)
    slot_count = owners * capacity
    target = tile_owner[:, 0]
    positions = jnp.arange(tile_count, dtype=jnp.int32)
    earlier = (target[:, None] == target[None, :]) & (positions[None, :] < positions[:, None])
    order_in = jnp.sum(earlier.astype(jnp.int32), axis=1)
    slot_of = target * capacity + order_in
    slot_ids = jnp.arange(slot_count, dtype=jnp.int32)
    matches = slot_of[:, None] == slot_ids[None, :]
    wanted_out = jnp.sum(jnp.where(matches, tile_block[:, None] + 1, 0), axis=0) - 1
    groups = lax.axis_size("narrow")
    me = lax.axis_index("narrow")
    own_rows = edge_row_count // groups
    own_degree = lax.dynamic_slice_in_dim(edge_degree, me * own_rows, own_rows)
    tile_of_slot = jnp.sum(jnp.where(matches, positions[:, None], 0), axis=0)
    wanted = lax.all_to_all(
        wanted_out.reshape(owners, capacity), "wide", split_axis=0, concat_axis=0, tiled=True
    ).reshape(slot_count)
    current = node_rows
    node_blocks = current.reshape(node_block_count, block_size, channels)
    degree_column = jnp.broadcast_to(own_degree.astype(jnp.float32)[:, None], (own_rows, channels))
    wanted, slot_of, tile_of_slot, degree_column = lax.optimization_barrier(
        (wanted, slot_of, tile_of_slot, degree_column)
    )
    filled = wanted >= 0
    rank = jnp.cumsum(filled.astype(jnp.int32)) - 1
    count = jnp.sum(filled.astype(jnp.int32)).reshape(1)
    order = jnp.sum(
        jnp.where(filled[None, :] & (rank[None, :] == slot_ids[:, None]), slot_ids[None, :], 0),
        axis=1,
    )
    picked = pick_rows(count, order, wanted, node_blocks)
    arrived = lax.all_to_all(
        picked.reshape(owners, capacity, block_size, channels),
        "wide",
        split_axis=0,
        concat_axis=0,
        tiled=True,
    )
    parts = tile_products(
        slot_of, arrived.reshape(slot_count, block_size, channels), tile_values, per_block
    )
    outgoing = round_kernel(
        tile_of_slot,
        parts,
        slot_count,
        tile_values,
        degree_column,
        w_in,
        w_out,
        groups,
        per_block,
    )
    returned = lax.all_to_all(
        outgoing.reshape(owners, capacity, block_size, channels),
        "wide",
        split_axis=0,
        concat_axis=0,
        tiled=True,
    )
    current = land_terms(
        count, order, wanted, returned.reshape(slot_count, block_size, channels), node_blocks
    ).reshape(node_block_count * block_size, channels)
    return current


def solution(mesh):
    return jax.shard_map(
        body,
        mesh=mesh,
        in_specs=(
            P(("wide", "narrow"), None),
            P(("wide", "narrow"), None, None),
            P(("wide", "narrow"), None),
            P(("wide", "narrow")),
            P("wide"),
            P(),
            P(),
        ),
        out_specs=P(("wide", "narrow"), None),
        check_vma=False,
    )
```

```python
import functools

import jax
import jax.numpy as jnp
from jax import lax
from jax.experimental import pallas as pl
from jax.experimental.pallas import tpu as pltpu
from jax.sharding import PartitionSpec as P
MESH = pl.DeviceIdType.MESH


def _round_kernel(groups, per_block, slot_of_ref, slot_tile_ref, arrived_ref, tiles_ref,
                  degree_ref, w_in_ref, w_out_ref, out_ref,
                  parts, inbox, stage, edge_out, terms, send_a, recv_a, send_b, recv_b):
    me = lax.axis_index("narrow")
    col = lax.axis_index("wide")
    tile_count = tiles_ref.shape[0]
    barrier = pltpu.get_barrier_semaphore()
    for k in range(1, groups):
        pl.semaphore_signal(barrier, inc=1, device_id=(col, lax.rem(me + k, groups)), device_id_type=MESH)

    for e in range(tile_count // per_block):
        acc = None
        for k in range(per_block):
            t = e * per_block + k
            rows = arrived_ref[slot_of_ref[t]]
            p = jnp.dot(tiles_ref[t], rows, preferred_element_type=jnp.float32)
            acc = p if acc is None else acc + p
        parts[e] = acc

    pl.semaphore_wait(barrier, groups - 1)

    def first(d):
        return pltpu.make_async_remote_copy(
            src_ref=parts.at[d], dst_ref=inbox.at[me], send_sem=send_a.at[d],
            recv_sem=recv_a.at[me], device_id=(col, d), device_id_type=MESH)

    for k in range(1, groups):
        first(lax.rem(me + k, groups)).start()
    total = parts[me]
    for k in range(1, groups):
        d = lax.rem(me + k, groups)
        s = lax.rem(me + groups - k, groups)
        first(d).wait_send()
        pltpu.make_async_remote_copy(
            src_ref=parts.at[s], dst_ref=inbox.at[s], send_sem=send_a.at[s],
            recv_sem=recv_a.at[s], device_id=(col, s), device_id_type=MESH).wait_recv()
        total = total + inbox[s]
    edge_in = (total / degree_ref[...]).astype(jnp.bfloat16)
    pre = jnp.dot(edge_in, w_in_ref[...], preferred_element_type=jnp.float32)
    hidden = (pre * jax.nn.sigmoid(pre)).astype(jnp.bfloat16)
    own = jnp.dot(hidden, w_out_ref[...], preferred_element_type=jnp.float32).astype(jnp.bfloat16)
    stage[...] = own
    edge_out[me] = own

    def second(d):
        return pltpu.make_async_remote_copy(
            src_ref=stage, dst_ref=edge_out.at[me], send_sem=send_b.at[d],
            recv_sem=recv_b.at[me], device_id=(col, d), device_id_type=MESH)

    for k in range(1, groups):
        second(lax.rem(me + k, groups)).start()

    def block_terms(e, block):
        for k in range(per_block):
            t = e * per_block + k
            term = lax.dot_general(
                tiles_ref[t], block, (((0,), (0,)), ((), ())),
                preferred_element_type=jnp.float32)
            terms[t] = term.astype(jnp.bfloat16)

    block_terms(me, own)
    for k in range(1, groups):
        d = lax.rem(me + k, groups)
        s = lax.rem(me + groups - k, groups)
        second(d).wait_send()
        pltpu.make_async_remote_copy(
            src_ref=stage, dst_ref=edge_out.at[s], send_sem=send_b.at[s],
            recv_sem=recv_b.at[s], device_id=(col, s), device_id_type=MESH).wait_recv()
        block_terms(s, edge_out[s])

    def place(slot, carry):
        out_ref[slot] = terms[slot_tile_ref[slot]]
        return carry

    lax.fori_loop(0, out_ref.shape[0], place, 0, unroll=8)


def round_kernel(slot_of, slot_tile, arrived, tiles, degree, w_in, w_out, groups, per_block):
    slots, rows, channels = arrived.shape
    vmem = pl.BlockSpec(memory_space=pltpu.VMEM)
    smem = pl.BlockSpec(memory_space=pltpu.SMEM)
    return pl.pallas_call(
        functools.partial(_round_kernel, groups, per_block),
        out_shape=jax.ShapeDtypeStruct((slots, rows, channels), jnp.bfloat16),
        in_specs=[smem, smem] + [vmem] * 5,
        out_specs=vmem,
        scratch_shapes=[
            pltpu.VMEM((groups, rows, channels), jnp.float32),
            pltpu.VMEM((groups, rows, channels), jnp.float32),
            pltpu.VMEM((rows, channels), jnp.bfloat16),
            pltpu.VMEM((groups, rows, channels), jnp.bfloat16),
            pltpu.VMEM(tiles.shape, jnp.bfloat16),
            pltpu.SemaphoreType.DMA((groups,)), pltpu.SemaphoreType.DMA((groups,)),
            pltpu.SemaphoreType.DMA((groups,)), pltpu.SemaphoreType.DMA((groups,)),
        ],
        compiler_params=pltpu.CompilerParams(
            collective_id=0, has_side_effects=True, vmem_limit_bytes=48 * 1024 * 1024),
    )(slot_of, slot_tile, arrived, tiles, degree, w_in, w_out)


def _pick_kernel(count_ref, order_ref, wanted_ref, rows_ref, out_ref, sems):
    last = rows_ref.shape[0] - 1

    def copy(i):
        slot = order_ref[i]
        block = jnp.clip(wanted_ref[slot], 0, last)
        return pltpu.make_async_copy(rows_ref.at[block], out_ref.at[slot], sems.at[i])

    def start(i, carry):
        copy(i).start()
        return carry

    def finish(i, carry):
        copy(i).wait()
        return carry

    lax.fori_loop(0, count_ref[0], start, 0)
    lax.fori_loop(0, count_ref[0], finish, 0)


def pick_rows(count, order, wanted, blocks):
    slots = wanted.shape[0]
    _, rows, channels = blocks.shape
    smem = pl.BlockSpec(memory_space=pltpu.SMEM)
    return pl.pallas_call(
        _pick_kernel,
        out_shape=jax.ShapeDtypeStruct((slots, rows, channels), blocks.dtype),
        in_specs=[smem, smem, smem, pl.BlockSpec(memory_space=pltpu.VMEM)],
        out_specs=pl.BlockSpec(memory_space=pl.ANY),
        scratch_shapes=[pltpu.SemaphoreType.DMA((slots,))],
    )(count, order, wanted, blocks)


def _land_kernel(count_ref, order_ref, wanted_ref, returned_ref, rows_ref, out_ref, buf, acc, sems):
    last = rows_ref.shape[0] - 1

    def copy(i):
        return pltpu.make_async_copy(returned_ref.at[order_ref[i]], buf.at[i], sems.at[i])

    def start(i, carry):
        copy(i).start()
        return carry

    lax.fori_loop(0, count_ref[0], start, 0)
    acc[...] = rows_ref[...].astype(jnp.float32)

    def add(i, carry):
        copy(i).wait()
        block = jnp.clip(wanted_ref[order_ref[i]], 0, last)
        acc[block] = acc[block] + buf[i].astype(jnp.float32)
        return carry

    lax.fori_loop(0, count_ref[0], add, 0)
    out_ref[...] = acc[...].astype(out_ref.dtype)


def land_terms(count, order, wanted, returned, blocks):
    slots, rows, channels = returned.shape
    smem = pl.BlockSpec(memory_space=pltpu.SMEM)
    return pl.pallas_call(
        _land_kernel,
        out_shape=jax.ShapeDtypeStruct(blocks.shape, blocks.dtype),
        in_specs=[smem, smem, smem, pl.BlockSpec(memory_space=pl.ANY), pl.BlockSpec(memory_space=pltpu.VMEM)],
        out_specs=pl.BlockSpec(memory_space=pltpu.VMEM),
        scratch_shapes=[
            pltpu.VMEM((slots, rows, channels), returned.dtype),
            pltpu.VMEM(blocks.shape, jnp.float32),
            pltpu.SemaphoreType.DMA((slots,)),
        ],
    )(count, order, wanted, returned, blocks)


def edge_network(summed, degrees, w_in, w_out):
    edge_in = (summed / degrees.astype(jnp.float32)[:, None]).astype(jnp.bfloat16)
    pre_act = jnp.dot(edge_in, w_in, preferred_element_type=jnp.float32)
    hidden = jax.nn.silu(pre_act).astype(jnp.bfloat16)
    return jnp.dot(hidden, w_out, preferred_element_type=jnp.float32).astype(jnp.bfloat16)


def body(node_rows, tile_values, tile_owner, tile_block, edge_degree, w_in, w_out):
    owners = lax.axis_size("wide")
    tile_count, block_size, _ = tile_values.shape
    channels = node_rows.shape[1]
    node_block_count = node_rows.shape[0] // block_size
    edge_row_count = edge_degree.shape[0]
    edge_blocks = edge_row_count // block_size
    per_block = tile_count // edge_blocks
    capacity = max(2, 2 * tile_count // owners)
    slot_count = owners * capacity
    target = tile_owner[:, 0]
    positions = jnp.arange(tile_count, dtype=jnp.int32)
    earlier = (target[:, None] == target[None, :]) & (positions[None, :] < positions[:, None])
    order_in = jnp.sum(earlier.astype(jnp.int32), axis=1)
    slot_of = target * capacity + order_in
    slot_ids = jnp.arange(slot_count, dtype=jnp.int32)
    matches = slot_of[:, None] == slot_ids[None, :]
    wanted_out = jnp.sum(jnp.where(matches, tile_block[:, None] + 1, 0), axis=0) - 1
    groups = lax.axis_size("narrow")
    me = lax.axis_index("narrow")
    own_rows = edge_row_count // groups
    own_degree = lax.dynamic_slice_in_dim(edge_degree, me * own_rows, own_rows)
    tile_of_slot = jnp.sum(jnp.where(matches, positions[:, None], 0), axis=0)
    wanted = lax.all_to_all(
        wanted_out.reshape(owners, capacity), "wide", split_axis=0, concat_axis=0, tiled=True
    ).reshape(slot_count)
    current = node_rows
    node_blocks = current.reshape(node_block_count, block_size, channels)
    degree_column = jnp.broadcast_to(own_degree.astype(jnp.float32)[:, None], (own_rows, channels))
    wanted, slot_of, tile_of_slot, degree_column = lax.optimization_barrier(
        (wanted, slot_of, tile_of_slot, degree_column)
    )
    filled = wanted >= 0
    before = filled[None, :] & (slot_ids[None, :] < slot_ids[:, None])
    rank = jnp.sum(before.astype(jnp.int32), axis=1)
    count = jnp.sum(filled.astype(jnp.int32)).reshape(1)
    order = jnp.sum(
        jnp.where(filled[None, :] & (rank[None, :] == slot_ids[:, None]), slot_ids[None, :], 0),
        axis=1,
    )
    picked = pick_rows(count, order, wanted, node_blocks)
    arrived = lax.all_to_all(
        picked.reshape(owners, capacity, block_size, channels),
        "wide",
        split_axis=0,
        concat_axis=0,
        tiled=True,
    )
    outgoing = round_kernel(
        slot_of,
        tile_of_slot,
        arrived.reshape(slot_count, block_size, channels),
        tile_values,
        degree_column,
        w_in,
        w_out,
        groups,
        per_block,
    )
    returned = lax.all_to_all(
        outgoing.reshape(owners, capacity, block_size, channels),
        "wide",
        split_axis=0,
        concat_axis=0,
        tiled=True,
    )
    current = land_terms(
        count, order, wanted, returned.reshape(slot_count, block_size, channels), node_blocks
    ).reshape(node_block_count * block_size, channels)
    return current


def solution(mesh):
    return jax.shard_map(
        body,
        mesh=mesh,
        in_specs=(
            P(("wide", "narrow"), None),
            P(("wide", "narrow"), None, None),
            P(("wide", "narrow"), None),
            P(("wide", "narrow")),
            P("wide"),
            P(),
            P(),
        ),
        out_specs=P(("wide", "narrow"), None),
        check_vma=False,
    )
```

```python
import functools

import jax
import jax.numpy as jnp
from jax import lax
from jax.experimental import pallas as pl
from jax.experimental.pallas import tpu as pltpu
from jax.sharding import PartitionSpec as P
MESH = pl.DeviceIdType.MESH


def _round_kernel(groups, per_block, slot_of_ref, slot_tile_ref, arrived_ref, tiles_ref,
                  degree_ref, w_in_ref, w_out_ref, out_ref,
                  parts, inbox, stage, edge_out, terms, send_a, recv_a, send_b, recv_b):
    me = lax.axis_index("narrow")
    col = lax.axis_index("wide")
    tile_count = tiles_ref.shape[0]
    barrier = pltpu.get_barrier_semaphore()
    for k in range(1, groups):
        pl.semaphore_signal(barrier, inc=1, device_id=(col, lax.rem(me + k, groups)), device_id_type=MESH)

    for e in range(tile_count // per_block):
        acc = None
        for k in range(per_block):
            t = e * per_block + k
            rows = arrived_ref[slot_of_ref[t]]
            p = jnp.dot(tiles_ref[t], rows, preferred_element_type=jnp.float32)
            acc = p if acc is None else acc + p
        parts[e] = acc

    pl.semaphore_wait(barrier, groups - 1)

    def first(d):
        return pltpu.make_async_remote_copy(
            src_ref=parts.at[d], dst_ref=inbox.at[me], send_sem=send_a.at[d],
            recv_sem=recv_a.at[me], device_id=(col, d), device_id_type=MESH)

    for k in range(1, groups):
        first(lax.rem(me + k, groups)).start()
    total = parts[me]
    for k in range(1, groups):
        d = lax.rem(me + k, groups)
        s = lax.rem(me + groups - k, groups)
        first(d).wait_send()
        pltpu.make_async_remote_copy(
            src_ref=parts.at[s], dst_ref=inbox.at[s], send_sem=send_a.at[s],
            recv_sem=recv_a.at[s], device_id=(col, s), device_id_type=MESH).wait_recv()
        total = total + inbox[s]
    edge_in = (total / degree_ref[...]).astype(jnp.bfloat16)
    pre = jnp.dot(edge_in, w_in_ref[...], preferred_element_type=jnp.float32)
    hidden = (pre * jax.nn.sigmoid(pre)).astype(jnp.bfloat16)
    own = jnp.dot(hidden, w_out_ref[...], preferred_element_type=jnp.float32).astype(jnp.bfloat16)
    stage[...] = own
    edge_out[me] = own

    def second(d):
        return pltpu.make_async_remote_copy(
            src_ref=stage, dst_ref=edge_out.at[me], send_sem=send_b.at[d],
            recv_sem=recv_b.at[me], device_id=(col, d), device_id_type=MESH)

    for k in range(1, groups):
        second(lax.rem(me + k, groups)).start()

    def block_terms(e, block):
        for k in range(per_block):
            t = e * per_block + k
            term = lax.dot_general(
                tiles_ref[t], block, (((0,), (0,)), ((), ())),
                preferred_element_type=jnp.float32)
            terms[t] = term.astype(jnp.bfloat16)

    block_terms(me, own)
    for k in range(1, groups):
        d = lax.rem(me + k, groups)
        s = lax.rem(me + groups - k, groups)
        second(d).wait_send()
        pltpu.make_async_remote_copy(
            src_ref=stage, dst_ref=edge_out.at[s], send_sem=send_b.at[s],
            recv_sem=recv_b.at[s], device_id=(col, s), device_id_type=MESH).wait_recv()
        block_terms(s, edge_out[s])

    def place(slot, carry):
        out_ref[slot] = terms[slot_tile_ref[slot]]
        return carry

    lax.fori_loop(0, out_ref.shape[0], place, 0, unroll=8)


def round_kernel(slot_of, slot_tile, arrived, tiles, degree, w_in, w_out, groups, per_block):
    slots, rows, channels = arrived.shape
    vmem = pl.BlockSpec(memory_space=pltpu.VMEM)
    smem = pl.BlockSpec(memory_space=pltpu.SMEM)
    return pl.pallas_call(
        functools.partial(_round_kernel, groups, per_block),
        out_shape=jax.ShapeDtypeStruct((slots, rows, channels), jnp.bfloat16),
        in_specs=[smem, smem] + [vmem] * 5,
        out_specs=vmem,
        scratch_shapes=[
            pltpu.VMEM((groups, rows, channels), jnp.float32),
            pltpu.VMEM((groups, rows, channels), jnp.float32),
            pltpu.VMEM((rows, channels), jnp.bfloat16),
            pltpu.VMEM((groups, rows, channels), jnp.bfloat16),
            pltpu.VMEM(tiles.shape, jnp.bfloat16),
            pltpu.SemaphoreType.DMA((groups,)), pltpu.SemaphoreType.DMA((groups,)),
            pltpu.SemaphoreType.DMA((groups,)), pltpu.SemaphoreType.DMA((groups,)),
        ],
        compiler_params=pltpu.CompilerParams(
            collective_id=0, has_side_effects=True, vmem_limit_bytes=48 * 1024 * 1024),
    )(slot_of, slot_tile, arrived, tiles, degree, w_in, w_out)


def _pick_kernel(count_ref, order_ref, wanted_ref, rows_ref, out_ref, sems):
    last = rows_ref.shape[0] - 1

    def copy(i):
        slot = order_ref[i]
        cap = wanted_ref.shape[2]
        block = jnp.clip(wanted_ref[slot // cap, 0, slot % cap], 0, last)
        return pltpu.make_async_copy(rows_ref.at[block], out_ref.at[slot], sems.at[i])

    def start(i, carry):
        copy(i).start()
        return carry

    def finish(i, carry):
        copy(i).wait()
        return carry

    lax.fori_loop(0, count_ref[0], start, 0)
    lax.fori_loop(0, count_ref[0], finish, 0)


def pick_rows(count, order, wanted, blocks):
    slots = wanted.shape[0] * wanted.shape[2]
    _, rows, channels = blocks.shape
    smem = pl.BlockSpec(memory_space=pltpu.SMEM)
    return pl.pallas_call(
        _pick_kernel,
        out_shape=jax.ShapeDtypeStruct((slots, rows, channels), blocks.dtype),
        in_specs=[smem, smem, smem, pl.BlockSpec(memory_space=pltpu.VMEM)],
        out_specs=pl.BlockSpec(memory_space=pl.ANY),
        scratch_shapes=[pltpu.SemaphoreType.DMA((slots,))],
    )(count, order, wanted, blocks)


def _land_kernel(count_ref, order_ref, wanted_ref, returned_ref, rows_ref, out_ref, buf, acc, sems):
    last = rows_ref.shape[0] - 1

    def copy(i):
        return pltpu.make_async_copy(returned_ref.at[order_ref[i]], buf.at[i], sems.at[i])

    def start(i, carry):
        copy(i).start()
        return carry

    lax.fori_loop(0, count_ref[0], start, 0)
    acc[...] = rows_ref[...].astype(jnp.float32)

    def add(i, carry):
        copy(i).wait()
        slot = order_ref[i]
        cap = wanted_ref.shape[2]
        block = jnp.clip(wanted_ref[slot // cap, 0, slot % cap], 0, last)
        acc[block] = acc[block] + buf[i].astype(jnp.float32)
        return carry

    lax.fori_loop(0, count_ref[0], add, 0)
    out_ref[...] = acc[...].astype(out_ref.dtype)


def land_terms(count, order, wanted, returned, blocks):
    slots, rows, channels = returned.shape
    smem = pl.BlockSpec(memory_space=pltpu.SMEM)
    return pl.pallas_call(
        _land_kernel,
        out_shape=jax.ShapeDtypeStruct(blocks.shape, blocks.dtype),
        in_specs=[smem, smem, smem, pl.BlockSpec(memory_space=pl.ANY), pl.BlockSpec(memory_space=pltpu.VMEM)],
        out_specs=pl.BlockSpec(memory_space=pltpu.VMEM),
        scratch_shapes=[
            pltpu.VMEM((slots, rows, channels), returned.dtype),
            pltpu.VMEM(blocks.shape, jnp.float32),
            pltpu.SemaphoreType.DMA((slots,)),
        ],
    )(count, order, wanted, returned, blocks)


def edge_network(summed, degrees, w_in, w_out):
    edge_in = (summed / degrees.astype(jnp.float32)[:, None]).astype(jnp.bfloat16)
    pre_act = jnp.dot(edge_in, w_in, preferred_element_type=jnp.float32)
    hidden = jax.nn.silu(pre_act).astype(jnp.bfloat16)
    return jnp.dot(hidden, w_out, preferred_element_type=jnp.float32).astype(jnp.bfloat16)


def body(node_rows, tile_values, tile_owner, tile_block, edge_degree, w_in, w_out):
    owners = lax.axis_size("wide")
    tile_count, block_size, _ = tile_values.shape
    channels = node_rows.shape[1]
    node_block_count = node_rows.shape[0] // block_size
    edge_row_count = edge_degree.shape[0]
    edge_blocks = edge_row_count // block_size
    per_block = tile_count // edge_blocks
    capacity = max(2, 2 * tile_count // owners)
    slot_count = owners * capacity
    target = tile_owner[:, 0]
    positions = jnp.arange(tile_count, dtype=jnp.int32)
    earlier = (target[:, None] == target[None, :]) & (positions[None, :] < positions[:, None])
    order_in = jnp.sum(earlier.astype(jnp.int32), axis=1)
    slot_of = target * capacity + order_in
    slot_ids = jnp.arange(slot_count, dtype=jnp.int32)
    matches = slot_of[:, None] == slot_ids[None, :]
    wanted_out = jnp.sum(jnp.where(matches, tile_block[:, None] + 1, 0), axis=0) - 1
    groups = lax.axis_size("narrow")
    me = lax.axis_index("narrow")
    own_rows = edge_row_count // groups
    own_degree = lax.dynamic_slice_in_dim(edge_degree, me * own_rows, own_rows)
    tile_of_slot = jnp.sum(jnp.where(matches, positions[:, None], 0), axis=0)
    asked = lax.all_to_all(
        wanted_out.reshape(owners, 1, capacity), "wide", split_axis=0, concat_axis=0, tiled=True
    )
    current = node_rows
    node_blocks = current.reshape(node_block_count, block_size, channels)
    degree_column = jnp.broadcast_to(own_degree.astype(jnp.float32)[:, None], (own_rows, channels))
    asked, slot_of, tile_of_slot, degree_column = lax.optimization_barrier(
        (asked, slot_of, tile_of_slot, degree_column)
    )
    filled = asked.reshape(slot_count) >= 0
    before = filled[None, :] & (slot_ids[None, :] < slot_ids[:, None])
    rank = jnp.sum(before.astype(jnp.int32), axis=1)
    count = jnp.sum(filled.astype(jnp.int32)).reshape(1)
    order = jnp.sum(
        jnp.where(filled[None, :] & (rank[None, :] == slot_ids[:, None]), slot_ids[None, :], 0),
        axis=1,
    )
    picked = pick_rows(count, order, asked, node_blocks)
    arrived = lax.all_to_all(
        picked.reshape(owners, capacity, block_size, channels),
        "wide",
        split_axis=0,
        concat_axis=0,
        tiled=True,
    )
    outgoing = round_kernel(
        slot_of,
        tile_of_slot,
        arrived.reshape(slot_count, block_size, channels),
        tile_values,
        degree_column,
        w_in,
        w_out,
        groups,
        per_block,
    )
    returned = lax.all_to_all(
        outgoing.reshape(owners, capacity, block_size, channels),
        "wide",
        split_axis=0,
        concat_axis=0,
        tiled=True,
    )
    current = land_terms(
        count, order, asked, returned.reshape(slot_count, block_size, channels), node_blocks
    ).reshape(node_block_count * block_size, channels)
    return current


def solution(mesh):
    return jax.shard_map(
        body,
        mesh=mesh,
        in_specs=(
            P(("wide", "narrow"), None),
            P(("wide", "narrow"), None, None),
            P(("wide", "narrow"), None),
            P(("wide", "narrow")),
            P("wide"),
            P(),
            P(),
        ),
        out_specs=P(("wide", "narrow"), None),
        check_vma=False,
    )
```

```python
import functools

import jax
import jax.numpy as jnp
from jax import lax
from jax.experimental import pallas as pl
from jax.experimental.pallas import tpu as pltpu
from jax.sharding import PartitionSpec as P
MESH = pl.DeviceIdType.MESH


def _round_kernel(groups, per_block, slot_of_ref, slot_tile_ref, arrived_ref, tiles_ref,
                  degree_ref, w_in_ref, w_out_ref, out_ref,
                  parts, inbox, stage, edge_out, terms, send_a, recv_a, send_b, recv_b):
    me = lax.axis_index("narrow")
    col = lax.axis_index("wide")
    tile_count = tiles_ref.shape[0]
    barrier = pltpu.get_barrier_semaphore()
    for k in range(1, groups):
        pl.semaphore_signal(barrier, inc=1, device_id=(col, lax.rem(me + k, groups)), device_id_type=MESH)

    for e in range(tile_count // per_block):
        acc = None
        for k in range(per_block):
            t = e * per_block + k
            rows = arrived_ref[slot_of_ref[t]]
            p = jnp.dot(tiles_ref[t], rows, preferred_element_type=jnp.float32)
            acc = p if acc is None else acc + p
        parts[e] = acc

    pl.semaphore_wait(barrier, groups - 1)

    def first(d):
        return pltpu.make_async_remote_copy(
            src_ref=parts.at[d], dst_ref=inbox.at[me], send_sem=send_a.at[d],
            recv_sem=recv_a.at[me], device_id=(col, d), device_id_type=MESH)

    for k in range(1, groups):
        first(lax.rem(me + k, groups)).start()
    total = parts[me]
    for k in range(1, groups):
        d = lax.rem(me + k, groups)
        s = lax.rem(me + groups - k, groups)
        first(d).wait_send()
        pltpu.make_async_remote_copy(
            src_ref=parts.at[s], dst_ref=inbox.at[s], send_sem=send_a.at[s],
            recv_sem=recv_a.at[s], device_id=(col, s), device_id_type=MESH).wait_recv()
        total = total + inbox[s]
    edge_in = (total / degree_ref[...]).astype(jnp.bfloat16)
    pre = jnp.dot(edge_in, w_in_ref[...], preferred_element_type=jnp.float32)
    hidden = (pre * jax.nn.sigmoid(pre)).astype(jnp.bfloat16)
    own = jnp.dot(hidden, w_out_ref[...], preferred_element_type=jnp.float32).astype(jnp.bfloat16)
    stage[...] = own
    edge_out[me] = own

    def second(d):
        return pltpu.make_async_remote_copy(
            src_ref=stage, dst_ref=edge_out.at[me], send_sem=send_b.at[d],
            recv_sem=recv_b.at[me], device_id=(col, d), device_id_type=MESH)

    for k in range(1, groups):
        second(lax.rem(me + k, groups)).start()

    def block_terms(e, block):
        for k in range(per_block):
            t = e * per_block + k
            term = lax.dot_general(
                tiles_ref[t], block, (((0,), (0,)), ((), ())),
                preferred_element_type=jnp.float32)
            terms[t] = term.astype(jnp.bfloat16)

    block_terms(me, own)
    for k in range(1, groups):
        d = lax.rem(me + k, groups)
        s = lax.rem(me + groups - k, groups)
        second(d).wait_send()
        pltpu.make_async_remote_copy(
            src_ref=stage, dst_ref=edge_out.at[s], send_sem=send_b.at[s],
            recv_sem=recv_b.at[s], device_id=(col, s), device_id_type=MESH).wait_recv()
        block_terms(s, edge_out[s])

    def place(slot, carry):
        out_ref[slot] = terms[slot_tile_ref[slot]]
        return carry

    lax.fori_loop(0, out_ref.shape[0], place, 0, unroll=8)


def round_kernel(slot_of, slot_tile, arrived, tiles, degree, w_in, w_out, groups, per_block):
    slots, rows, channels = arrived.shape
    vmem = pl.BlockSpec(memory_space=pltpu.VMEM)
    smem = pl.BlockSpec(memory_space=pltpu.SMEM)
    return pl.pallas_call(
        functools.partial(_round_kernel, groups, per_block),
        out_shape=jax.ShapeDtypeStruct((slots, rows, channels), jnp.bfloat16),
        in_specs=[smem, smem] + [vmem] * 5,
        out_specs=vmem,
        scratch_shapes=[
            pltpu.VMEM((groups, rows, channels), jnp.float32),
            pltpu.VMEM((groups, rows, channels), jnp.float32),
            pltpu.VMEM((rows, channels), jnp.bfloat16),
            pltpu.VMEM((groups, rows, channels), jnp.bfloat16),
            pltpu.VMEM(tiles.shape, jnp.bfloat16),
            pltpu.SemaphoreType.DMA((groups,)), pltpu.SemaphoreType.DMA((groups,)),
            pltpu.SemaphoreType.DMA((groups,)), pltpu.SemaphoreType.DMA((groups,)),
        ],
        compiler_params=pltpu.CompilerParams(
            collective_id=0, has_side_effects=True, vmem_limit_bytes=48 * 1024 * 1024),
    )(slot_of, slot_tile, arrived, tiles, degree, w_in, w_out)


def _pick_kernel(count_ref, order_ref, wanted_ref, rows_ref, out_ref, sems):
    last = rows_ref.shape[0] - 1

    def copy(i):
        slot = order_ref[i]
        cap = wanted_ref.shape[2]
        block = jnp.clip(wanted_ref[slot // cap, 0, slot % cap], 0, last)
        return pltpu.make_async_copy(rows_ref.at[block], out_ref.at[slot], sems.at[i])

    def start(i, carry):
        copy(i).start()
        return carry

    def finish(i, carry):
        copy(i).wait()
        return carry

    lax.fori_loop(0, count_ref[0], start, 0)
    lax.fori_loop(0, count_ref[0], finish, 0)


def pick_rows(count, order, wanted, blocks):
    slots = wanted.shape[0] * wanted.shape[2]
    _, rows, channels = blocks.shape
    smem = pl.BlockSpec(memory_space=pltpu.SMEM)
    return pl.pallas_call(
        _pick_kernel,
        out_shape=jax.ShapeDtypeStruct((slots, rows, channels), blocks.dtype),
        in_specs=[smem, smem, smem, pl.BlockSpec(memory_space=pltpu.HBM)],
        out_specs=pl.BlockSpec(memory_space=pl.ANY),
        scratch_shapes=[pltpu.SemaphoreType.DMA((slots,))],
    )(count, order, wanted, blocks)


def _land_kernel(count_ref, order_ref, wanted_ref, returned_ref, rows_ref, out_ref, buf, acc, sems):
    last = rows_ref.shape[0] - 1

    def copy(i):
        return pltpu.make_async_copy(returned_ref.at[order_ref[i]], buf.at[i], sems.at[i])

    def start(i, carry):
        copy(i).start()
        return carry

    lax.fori_loop(0, count_ref[0], start, 0)
    acc[...] = rows_ref[...].astype(jnp.float32)

    def add(i, carry):
        copy(i).wait()
        slot = order_ref[i]
        cap = wanted_ref.shape[2]
        block = jnp.clip(wanted_ref[slot // cap, 0, slot % cap], 0, last)
        acc[block] = acc[block] + buf[i].astype(jnp.float32)
        return carry

    lax.fori_loop(0, count_ref[0], add, 0)
    out_ref[...] = acc[...].astype(out_ref.dtype)


def land_terms(count, order, wanted, returned, blocks):
    slots, rows, channels = returned.shape
    smem = pl.BlockSpec(memory_space=pltpu.SMEM)
    return pl.pallas_call(
        _land_kernel,
        out_shape=jax.ShapeDtypeStruct(blocks.shape, blocks.dtype),
        in_specs=[smem, smem, smem, pl.BlockSpec(memory_space=pl.ANY), pl.BlockSpec(memory_space=pltpu.VMEM)],
        out_specs=pl.BlockSpec(memory_space=pltpu.VMEM),
        scratch_shapes=[
            pltpu.VMEM((slots, rows, channels), returned.dtype),
            pltpu.VMEM(blocks.shape, jnp.float32),
            pltpu.SemaphoreType.DMA((slots,)),
        ],
    )(count, order, wanted, returned, blocks)


def edge_network(summed, degrees, w_in, w_out):
    edge_in = (summed / degrees.astype(jnp.float32)[:, None]).astype(jnp.bfloat16)
    pre_act = jnp.dot(edge_in, w_in, preferred_element_type=jnp.float32)
    hidden = jax.nn.silu(pre_act).astype(jnp.bfloat16)
    return jnp.dot(hidden, w_out, preferred_element_type=jnp.float32).astype(jnp.bfloat16)


def body(node_rows, tile_values, tile_owner, tile_block, edge_degree, w_in, w_out):
    owners = lax.axis_size("wide")
    tile_count, block_size, _ = tile_values.shape
    channels = node_rows.shape[1]
    node_block_count = node_rows.shape[0] // block_size
    edge_row_count = edge_degree.shape[0]
    edge_blocks = edge_row_count // block_size
    per_block = tile_count // edge_blocks
    capacity = max(2, 2 * tile_count // owners)
    slot_count = owners * capacity
    target = tile_owner[:, 0]
    positions = jnp.arange(tile_count, dtype=jnp.int32)
    earlier = (target[:, None] == target[None, :]) & (positions[None, :] < positions[:, None])
    order_in = jnp.sum(earlier.astype(jnp.int32), axis=1)
    slot_of = target * capacity + order_in
    slot_ids = jnp.arange(slot_count, dtype=jnp.int32)
    matches = slot_of[:, None] == slot_ids[None, :]
    wanted_out = jnp.sum(jnp.where(matches, tile_block[:, None] + 1, 0), axis=0) - 1
    groups = lax.axis_size("narrow")
    me = lax.axis_index("narrow")
    own_rows = edge_row_count // groups
    own_degree = lax.dynamic_slice_in_dim(edge_degree, me * own_rows, own_rows)
    tile_of_slot = jnp.sum(jnp.where(matches, positions[:, None], 0), axis=0)
    asked = lax.all_to_all(
        wanted_out.reshape(owners, 1, capacity), "wide", split_axis=0, concat_axis=0, tiled=True
    )
    current = node_rows
    node_blocks = current.reshape(node_block_count, block_size, channels)
    degree_column = jnp.broadcast_to(own_degree.astype(jnp.float32)[:, None], (own_rows, channels))
    asked, slot_of, tile_of_slot, degree_column = lax.optimization_barrier(
        (asked, slot_of, tile_of_slot, degree_column)
    )
    filled = asked.reshape(slot_count) >= 0
    before = filled[None, :] & (slot_ids[None, :] < slot_ids[:, None])
    rank = jnp.sum(before.astype(jnp.int32), axis=1)
    count = jnp.sum(filled.astype(jnp.int32)).reshape(1)
    order = jnp.sum(
        jnp.where(filled[None, :] & (rank[None, :] == slot_ids[:, None]), slot_ids[None, :], 0),
        axis=1,
    )
    picked = pick_rows(count, order, asked, node_blocks)
    arrived = lax.all_to_all(
        picked.reshape(owners, capacity, block_size, channels),
        "wide",
        split_axis=0,
        concat_axis=0,
        tiled=True,
    )
    outgoing = round_kernel(
        slot_of,
        tile_of_slot,
        arrived.reshape(slot_count, block_size, channels),
        tile_values,
        degree_column,
        w_in,
        w_out,
        groups,
        per_block,
    )
    returned = lax.all_to_all(
        outgoing.reshape(owners, capacity, block_size, channels),
        "wide",
        split_axis=0,
        concat_axis=0,
        tiled=True,
    )
    current = land_terms(
        count, order, asked, returned.reshape(slot_count, block_size, channels), node_blocks
    ).reshape(node_block_count * block_size, channels)
    return current


def solution(mesh):
    return jax.shard_map(
        body,
        mesh=mesh,
        in_specs=(
            P(("wide", "narrow"), None),
            P(("wide", "narrow"), None, None),
            P(("wide", "narrow"), None),
            P(("wide", "narrow")),
            P("wide"),
            P(),
            P(),
        ),
        out_specs=P(("wide", "narrow"), None),
        check_vma=False,
    )
```

```python
import functools

import jax
import jax.numpy as jnp
from jax import lax
from jax.experimental import pallas as pl
from jax.experimental.pallas import tpu as pltpu
from jax.sharding import PartitionSpec as P
MESH = pl.DeviceIdType.MESH


def _round_kernel(groups, per_block, slot_of_ref, slot_tile_ref, arrived_ref, tiles_ref,
                  degree_ref, w_in_ref, w_out_ref, out_ref,
                  parts, inbox, stage, edge_out, terms, send_a, recv_a, send_b, recv_b):
    me = lax.axis_index("narrow")
    col = lax.axis_index("wide")
    tile_count = tiles_ref.shape[0]
    barrier = pltpu.get_barrier_semaphore()
    for k in range(1, groups):
        pl.semaphore_signal(barrier, inc=1, device_id=(col, lax.rem(me + k, groups)), device_id_type=MESH)

    for e in range(tile_count // per_block):
        acc = None
        for k in range(per_block):
            t = e * per_block + k
            rows = arrived_ref[slot_of_ref[t]]
            p = jnp.dot(tiles_ref[t], rows, preferred_element_type=jnp.float32)
            acc = p if acc is None else acc + p
        parts[e] = acc

    pl.semaphore_wait(barrier, groups - 1)

    def first(d):
        return pltpu.make_async_remote_copy(
            src_ref=parts.at[d], dst_ref=inbox.at[me], send_sem=send_a.at[d],
            recv_sem=recv_a.at[me], device_id=(col, d), device_id_type=MESH)

    for k in range(1, groups):
        first(lax.rem(me + k, groups)).start()
    total = parts[me]
    for k in range(1, groups):
        d = lax.rem(me + k, groups)
        s = lax.rem(me + groups - k, groups)
        first(d).wait_send()
        pltpu.make_async_remote_copy(
            src_ref=parts.at[s], dst_ref=inbox.at[s], send_sem=send_a.at[s],
            recv_sem=recv_a.at[s], device_id=(col, s), device_id_type=MESH).wait_recv()
        total = total + inbox[s]
    edge_in = (total / degree_ref[...]).astype(jnp.bfloat16)
    pre = jnp.dot(edge_in, w_in_ref[...], preferred_element_type=jnp.float32)
    hidden = (pre * jax.nn.sigmoid(pre)).astype(jnp.bfloat16)
    own = jnp.dot(hidden, w_out_ref[...], preferred_element_type=jnp.float32).astype(jnp.bfloat16)
    stage[...] = own
    edge_out[me] = own

    def second(d):
        return pltpu.make_async_remote_copy(
            src_ref=stage, dst_ref=edge_out.at[me], send_sem=send_b.at[d],
            recv_sem=recv_b.at[me], device_id=(col, d), device_id_type=MESH)

    for k in range(1, groups):
        second(lax.rem(me + k, groups)).start()

    def block_terms(e, block):
        for k in range(per_block):
            t = e * per_block + k
            term = lax.dot_general(
                tiles_ref[t], block, (((0,), (0,)), ((), ())),
                preferred_element_type=jnp.float32)
            terms[t] = term.astype(jnp.bfloat16)

    block_terms(me, own)
    for k in range(1, groups):
        d = lax.rem(me + k, groups)
        s = lax.rem(me + groups - k, groups)
        second(d).wait_send()
        pltpu.make_async_remote_copy(
            src_ref=stage, dst_ref=edge_out.at[s], send_sem=send_b.at[s],
            recv_sem=recv_b.at[s], device_id=(col, s), device_id_type=MESH).wait_recv()
        block_terms(s, edge_out[s])

    def place(slot, carry):
        out_ref[slot] = terms[slot_tile_ref[slot]]
        return carry

    lax.fori_loop(0, out_ref.shape[0], place, 0, unroll=8)


def round_kernel(slot_of, slot_tile, arrived, tiles, degree, w_in, w_out, groups, per_block):
    slots, rows, channels = arrived.shape
    vmem = pl.BlockSpec(memory_space=pltpu.VMEM)
    smem = pl.BlockSpec(memory_space=pltpu.SMEM)
    return pl.pallas_call(
        functools.partial(_round_kernel, groups, per_block),
        out_shape=jax.ShapeDtypeStruct((slots, rows, channels), jnp.bfloat16),
        in_specs=[smem, smem] + [vmem] * 5,
        out_specs=vmem,
        scratch_shapes=[
            pltpu.VMEM((groups, rows, channels), jnp.float32),
            pltpu.VMEM((groups, rows, channels), jnp.float32),
            pltpu.VMEM((rows, channels), jnp.bfloat16),
            pltpu.VMEM((groups, rows, channels), jnp.bfloat16),
            pltpu.VMEM(tiles.shape, jnp.bfloat16),
            pltpu.SemaphoreType.DMA((groups,)), pltpu.SemaphoreType.DMA((groups,)),
            pltpu.SemaphoreType.DMA((groups,)), pltpu.SemaphoreType.DMA((groups,)),
        ],
        compiler_params=pltpu.CompilerParams(
            collective_id=0, has_side_effects=True, vmem_limit_bytes=48 * 1024 * 1024),
    )(slot_of, slot_tile, arrived, tiles, degree, w_in, w_out)


def _pick_kernel(count_ref, order_ref, wanted_ref, rows_ref, out_ref, sems):
    last = rows_ref.shape[0] - 1

    def copy(i):
        slot = order_ref[i]
        cap = wanted_ref.shape[2]
        block = jnp.clip(wanted_ref[slot // cap, 0, slot % cap], 0, last)
        return pltpu.make_async_copy(rows_ref.at[block], out_ref.at[slot], sems.at[i])

    def start(i, carry):
        copy(i).start()
        return carry

    def finish(i, carry):
        copy(i).wait()
        return carry

    lax.fori_loop(0, count_ref[0], start, 0)
    lax.fori_loop(0, count_ref[0], finish, 0)


def pick_rows(count, order, wanted, blocks):
    slots = wanted.shape[0] * wanted.shape[2]
    _, rows, channels = blocks.shape
    smem = pl.BlockSpec(memory_space=pltpu.SMEM)
    return pl.pallas_call(
        _pick_kernel,
        out_shape=jax.ShapeDtypeStruct((slots, rows, channels), blocks.dtype),
        in_specs=[smem, smem, smem, pl.BlockSpec(memory_space=pltpu.VMEM)],
        out_specs=pl.BlockSpec(memory_space=pl.ANY),
        scratch_shapes=[pltpu.SemaphoreType.DMA((slots,))],
    )(count, order, wanted, blocks)


def _land_kernel(count_ref, order_ref, wanted_ref, returned_ref, rows_hbm, out_ref, buf, acc, sems,
                 rows_ref, rows_sem):
    last = rows_ref.shape[0] - 1

    def copy(i):
        return pltpu.make_async_copy(returned_ref.at[order_ref[i]], buf.at[i], sems.at[i])

    def start(i, carry):
        copy(i).start()
        return carry

    rows_in = pltpu.make_async_copy(rows_hbm, rows_ref, rows_sem)
    rows_in.start()
    lax.fori_loop(0, count_ref[0], start, 0)
    rows_in.wait()
    acc[...] = rows_ref[...].astype(jnp.float32)

    def add(i, carry):
        copy(i).wait()
        slot = order_ref[i]
        cap = wanted_ref.shape[2]
        block = jnp.clip(wanted_ref[slot // cap, 0, slot % cap], 0, last)
        acc[block] = acc[block] + buf[i].astype(jnp.float32)
        return carry

    lax.fori_loop(0, count_ref[0], add, 0)
    out_ref[...] = acc[...].astype(out_ref.dtype)


def land_terms(count, order, wanted, returned, blocks):
    slots, rows, channels = returned.shape
    smem = pl.BlockSpec(memory_space=pltpu.SMEM)
    return pl.pallas_call(
        _land_kernel,
        out_shape=jax.ShapeDtypeStruct(blocks.shape, blocks.dtype),
        in_specs=[smem, smem, smem, pl.BlockSpec(memory_space=pl.ANY), pl.BlockSpec(memory_space=pl.ANY)],
        out_specs=pl.BlockSpec(memory_space=pltpu.VMEM),
        scratch_shapes=[
            pltpu.VMEM((slots, rows, channels), returned.dtype),
            pltpu.VMEM(blocks.shape, jnp.float32),
            pltpu.SemaphoreType.DMA((slots,)),
            pltpu.VMEM(blocks.shape, blocks.dtype),
            pltpu.SemaphoreType.DMA,
        ],
    )(count, order, wanted, returned, blocks)


def edge_network(summed, degrees, w_in, w_out):
    edge_in = (summed / degrees.astype(jnp.float32)[:, None]).astype(jnp.bfloat16)
    pre_act = jnp.dot(edge_in, w_in, preferred_element_type=jnp.float32)
    hidden = jax.nn.silu(pre_act).astype(jnp.bfloat16)
    return jnp.dot(hidden, w_out, preferred_element_type=jnp.float32).astype(jnp.bfloat16)


def body(node_rows, tile_values, tile_owner, tile_block, edge_degree, w_in, w_out):
    owners = lax.axis_size("wide")
    tile_count, block_size, _ = tile_values.shape
    channels = node_rows.shape[1]
    node_block_count = node_rows.shape[0] // block_size
    edge_row_count = edge_degree.shape[0]
    edge_blocks = edge_row_count // block_size
    per_block = tile_count // edge_blocks
    capacity = max(2, 2 * tile_count // owners)
    slot_count = owners * capacity
    target = tile_owner[:, 0]
    positions = jnp.arange(tile_count, dtype=jnp.int32)
    earlier = (target[:, None] == target[None, :]) & (positions[None, :] < positions[:, None])
    order_in = jnp.sum(earlier.astype(jnp.int32), axis=1)
    slot_of = target * capacity + order_in
    slot_ids = jnp.arange(slot_count, dtype=jnp.int32)
    matches = slot_of[:, None] == slot_ids[None, :]
    wanted_out = jnp.sum(jnp.where(matches, tile_block[:, None] + 1, 0), axis=0) - 1
    groups = lax.axis_size("narrow")
    me = lax.axis_index("narrow")
    own_rows = edge_row_count // groups
    own_degree = lax.dynamic_slice_in_dim(edge_degree, me * own_rows, own_rows)
    tile_of_slot = jnp.sum(jnp.where(matches, positions[:, None], 0), axis=0)
    asked = lax.all_to_all(
        wanted_out.reshape(owners, 1, capacity), "wide", split_axis=0, concat_axis=0, tiled=True
    )
    current = node_rows
    node_blocks = current.reshape(node_block_count, block_size, channels)
    degree_column = jnp.broadcast_to(own_degree.astype(jnp.float32)[:, None], (own_rows, channels))
    asked, slot_of, tile_of_slot, degree_column = lax.optimization_barrier(
        (asked, slot_of, tile_of_slot, degree_column)
    )
    filled = asked.reshape(slot_count) >= 0
    before = filled[None, :] & (slot_ids[None, :] < slot_ids[:, None])
    rank = jnp.sum(before.astype(jnp.int32), axis=1)
    count = jnp.sum(filled.astype(jnp.int32)).reshape(1)
    order = jnp.sum(
        jnp.where(filled[None, :] & (rank[None, :] == slot_ids[:, None]), slot_ids[None, :], 0),
        axis=1,
    )
    picked = pick_rows(count, order, asked, node_blocks)
    arrived = lax.all_to_all(
        picked.reshape(owners, capacity, block_size, channels),
        "wide",
        split_axis=0,
        concat_axis=0,
        tiled=True,
    )
    outgoing = round_kernel(
        slot_of,
        tile_of_slot,
        arrived.reshape(slot_count, block_size, channels),
        tile_values,
        degree_column,
        w_in,
        w_out,
        groups,
        per_block,
    )
    returned = lax.all_to_all(
        outgoing.reshape(owners, capacity, block_size, channels),
        "wide",
        split_axis=0,
        concat_axis=0,
        tiled=True,
    )
    current = land_terms(
        count, order, asked, returned.reshape(slot_count, block_size, channels), node_blocks
    ).reshape(node_block_count * block_size, channels)
    return current


def solution(mesh):
    return jax.shard_map(
        body,
        mesh=mesh,
        in_specs=(
            P(("wide", "narrow"), None),
            P(("wide", "narrow"), None, None),
            P(("wide", "narrow"), None),
            P(("wide", "narrow")),
            P("wide"),
            P(),
            P(),
        ),
        out_specs=P(("wide", "narrow"), None),
        check_vma=False,
    )
```

```python
import functools

import jax
import jax.numpy as jnp
from jax import lax
from jax.experimental import pallas as pl
from jax.experimental.pallas import tpu as pltpu
from jax.sharding import PartitionSpec as P
MESH = pl.DeviceIdType.MESH


def _round_kernel(groups, per_block, slot_of_ref, slot_tile_ref, arrived_ref, tiles_ref,
                  degree_ref, w_in_ref, w_out_ref, out_ref,
                  parts, inbox, stage, edge_out, terms, send_a, recv_a, send_b, recv_b):
    me = lax.axis_index("narrow")
    col = lax.axis_index("wide")
    tile_count = tiles_ref.shape[0]
    barrier = pltpu.get_barrier_semaphore()
    for k in range(1, groups):
        pl.semaphore_signal(barrier, inc=1, device_id=(col, lax.rem(me + k, groups)), device_id_type=MESH)

    for e in range(tile_count // per_block):
        acc = None
        for k in range(per_block):
            t = e * per_block + k
            rows = arrived_ref[slot_of_ref[t]]
            p = jnp.dot(tiles_ref[t], rows, preferred_element_type=jnp.float32)
            acc = p if acc is None else acc + p
        parts[e] = acc

    pl.semaphore_wait(barrier, groups - 1)

    def first(d):
        return pltpu.make_async_remote_copy(
            src_ref=parts.at[d], dst_ref=inbox.at[me], send_sem=send_a.at[d],
            recv_sem=recv_a.at[me], device_id=(col, d), device_id_type=MESH)

    for k in range(1, groups):
        first(lax.rem(me + k, groups)).start()
    total = parts[me]
    for k in range(1, groups):
        d = lax.rem(me + k, groups)
        s = lax.rem(me + groups - k, groups)
        first(d).wait_send()
        pltpu.make_async_remote_copy(
            src_ref=parts.at[s], dst_ref=inbox.at[s], send_sem=send_a.at[s],
            recv_sem=recv_a.at[s], device_id=(col, s), device_id_type=MESH).wait_recv()
        total = total + inbox[s]
    edge_in = (total / degree_ref[...]).astype(jnp.bfloat16)
    pre = jnp.dot(edge_in, w_in_ref[...], preferred_element_type=jnp.float32)
    hidden = (pre * jax.nn.sigmoid(pre)).astype(jnp.bfloat16)
    own = jnp.dot(hidden, w_out_ref[...], preferred_element_type=jnp.float32).astype(jnp.bfloat16)
    stage[...] = own
    edge_out[me] = own

    def second(d):
        return pltpu.make_async_remote_copy(
            src_ref=stage, dst_ref=edge_out.at[me], send_sem=send_b.at[d],
            recv_sem=recv_b.at[me], device_id=(col, d), device_id_type=MESH)

    for k in range(1, groups):
        second(lax.rem(me + k, groups)).start()

    def block_terms(e, block):
        for k in range(per_block):
            t = e * per_block + k
            term = lax.dot_general(
                tiles_ref[t], block, (((0,), (0,)), ((), ())),
                preferred_element_type=jnp.float32)
            terms[t] = term.astype(jnp.bfloat16)

    block_terms(me, own)
    for k in range(1, groups):
        d = lax.rem(me + k, groups)
        s = lax.rem(me + groups - k, groups)
        second(d).wait_send()
        pltpu.make_async_remote_copy(
            src_ref=stage, dst_ref=edge_out.at[s], send_sem=send_b.at[s],
            recv_sem=recv_b.at[s], device_id=(col, s), device_id_type=MESH).wait_recv()
        block_terms(s, edge_out[s])

    def place(slot, carry):
        out_ref[slot] = terms[slot_tile_ref[slot]]
        return carry

    lax.fori_loop(0, out_ref.shape[0], place, 0, unroll=8)


def round_kernel(slot_of, slot_tile, arrived, tiles, degree, w_in, w_out, groups, per_block):
    slots, rows, channels = arrived.shape
    vmem = pl.BlockSpec(memory_space=pltpu.VMEM)
    smem = pl.BlockSpec(memory_space=pltpu.SMEM)
    return pl.pallas_call(
        functools.partial(_round_kernel, groups, per_block),
        out_shape=jax.ShapeDtypeStruct((slots, rows, channels), jnp.bfloat16),
        in_specs=[smem, smem] + [vmem] * 5,
        out_specs=vmem,
        scratch_shapes=[
            pltpu.VMEM((groups, rows, channels), jnp.float32),
            pltpu.VMEM((groups, rows, channels), jnp.float32),
            pltpu.VMEM((rows, channels), jnp.bfloat16),
            pltpu.VMEM((groups, rows, channels), jnp.bfloat16),
            pltpu.VMEM(tiles.shape, jnp.bfloat16),
            pltpu.SemaphoreType.DMA((groups,)), pltpu.SemaphoreType.DMA((groups,)),
            pltpu.SemaphoreType.DMA((groups,)), pltpu.SemaphoreType.DMA((groups,)),
        ],
        compiler_params=pltpu.CompilerParams(
            collective_id=0, has_side_effects=True, vmem_limit_bytes=24 * 1024 * 1024),
    )(slot_of, slot_tile, arrived, tiles, degree, w_in, w_out)


def _pick_kernel(count_ref, order_ref, wanted_ref, rows_ref, out_ref, sems):
    last = rows_ref.shape[0] - 1

    def copy(i):
        slot = order_ref[i]
        cap = wanted_ref.shape[2]
        block = jnp.clip(wanted_ref[slot // cap, 0, slot % cap], 0, last)
        return pltpu.make_async_copy(rows_ref.at[block], out_ref.at[slot], sems.at[i])

    def start(i, carry):
        copy(i).start()
        return carry

    def finish(i, carry):
        copy(i).wait()
        return carry

    lax.fori_loop(0, count_ref[0], start, 0)
    lax.fori_loop(0, count_ref[0], finish, 0)


def pick_rows(count, order, wanted, blocks):
    slots = wanted.shape[0] * wanted.shape[2]
    _, rows, channels = blocks.shape
    smem = pl.BlockSpec(memory_space=pltpu.SMEM)
    return pl.pallas_call(
        _pick_kernel,
        out_shape=jax.ShapeDtypeStruct((slots, rows, channels), blocks.dtype),
        in_specs=[smem, smem, smem, pl.BlockSpec(memory_space=pltpu.VMEM)],
        out_specs=pl.BlockSpec(memory_space=pl.ANY),
        scratch_shapes=[pltpu.SemaphoreType.DMA((slots,))],
    )(count, order, wanted, blocks)


def _land_kernel(count_ref, order_ref, wanted_ref, returned_ref, rows_ref, out_ref, buf, acc, sems):
    last = rows_ref.shape[0] - 1

    def copy(i):
        return pltpu.make_async_copy(returned_ref.at[order_ref[i]], buf.at[i], sems.at[i])

    def start(i, carry):
        copy(i).start()
        return carry

    lax.fori_loop(0, count_ref[0], start, 0)
    acc[...] = rows_ref[...].astype(jnp.float32)

    def add(i, carry):
        copy(i).wait()
        slot = order_ref[i]
        cap = wanted_ref.shape[2]
        block = jnp.clip(wanted_ref[slot // cap, 0, slot % cap], 0, last)
        acc[block] = acc[block] + buf[i].astype(jnp.float32)
        return carry

    lax.fori_loop(0, count_ref[0], add, 0)
    out_ref[...] = acc[...].astype(out_ref.dtype)


def land_terms(count, order, wanted, returned, blocks):
    slots, rows, channels = returned.shape
    smem = pl.BlockSpec(memory_space=pltpu.SMEM)
    return pl.pallas_call(
        _land_kernel,
        out_shape=jax.ShapeDtypeStruct(blocks.shape, blocks.dtype),
        in_specs=[smem, smem, smem, pl.BlockSpec(memory_space=pl.ANY), pl.BlockSpec(memory_space=pltpu.VMEM)],
        out_specs=pl.BlockSpec(memory_space=pltpu.VMEM),
        scratch_shapes=[
            pltpu.VMEM((slots, rows, channels), returned.dtype),
            pltpu.VMEM(blocks.shape, jnp.float32),
            pltpu.SemaphoreType.DMA((slots,)),
        ],
    )(count, order, wanted, returned, blocks)


def edge_network(summed, degrees, w_in, w_out):
    edge_in = (summed / degrees.astype(jnp.float32)[:, None]).astype(jnp.bfloat16)
    pre_act = jnp.dot(edge_in, w_in, preferred_element_type=jnp.float32)
    hidden = jax.nn.silu(pre_act).astype(jnp.bfloat16)
    return jnp.dot(hidden, w_out, preferred_element_type=jnp.float32).astype(jnp.bfloat16)


def body(node_rows, tile_values, tile_owner, tile_block, edge_degree, w_in, w_out):
    owners = lax.axis_size("wide")
    tile_count, block_size, _ = tile_values.shape
    channels = node_rows.shape[1]
    node_block_count = node_rows.shape[0] // block_size
    edge_row_count = edge_degree.shape[0]
    edge_blocks = edge_row_count // block_size
    per_block = tile_count // edge_blocks
    capacity = max(2, 2 * tile_count // owners)
    slot_count = owners * capacity
    target = tile_owner[:, 0]
    positions = jnp.arange(tile_count, dtype=jnp.int32)
    earlier = (target[:, None] == target[None, :]) & (positions[None, :] < positions[:, None])
    order_in = jnp.sum(earlier.astype(jnp.int32), axis=1)
    slot_of = target * capacity + order_in
    slot_ids = jnp.arange(slot_count, dtype=jnp.int32)
    matches = slot_of[:, None] == slot_ids[None, :]
    wanted_out = jnp.sum(jnp.where(matches, tile_block[:, None] + 1, 0), axis=0) - 1
    groups = lax.axis_size("narrow")
    me = lax.axis_index("narrow")
    own_rows = edge_row_count // groups
    own_degree = lax.dynamic_slice_in_dim(edge_degree, me * own_rows, own_rows)
    tile_of_slot = jnp.sum(jnp.where(matches, positions[:, None], 0), axis=0)
    asked = lax.all_to_all(
        wanted_out.reshape(owners, 1, capacity), "wide", split_axis=0, concat_axis=0, tiled=True
    )
    current = node_rows
    node_blocks = current.reshape(node_block_count, block_size, channels)
    degree_column = jnp.broadcast_to(own_degree.astype(jnp.float32)[:, None], (own_rows, channels))
    asked, slot_of, tile_of_slot, degree_column = lax.optimization_barrier(
        (asked, slot_of, tile_of_slot, degree_column)
    )
    filled = asked.reshape(slot_count) >= 0
    before = filled[None, :] & (slot_ids[None, :] < slot_ids[:, None])
    rank = jnp.sum(before.astype(jnp.int32), axis=1)
    count = jnp.sum(filled.astype(jnp.int32)).reshape(1)
    order = jnp.sum(
        jnp.where(filled[None, :] & (rank[None, :] == slot_ids[:, None]), slot_ids[None, :], 0),
        axis=1,
    )
    picked = pick_rows(count, order, asked, node_blocks)
    arrived = lax.all_to_all(
        picked.reshape(owners, capacity, block_size, channels),
        "wide",
        split_axis=0,
        concat_axis=0,
        tiled=True,
    )
    outgoing = round_kernel(
        slot_of,
        tile_of_slot,
        arrived.reshape(slot_count, block_size, channels),
        tile_values,
        degree_column,
        w_in,
        w_out,
        groups,
        per_block,
    )
    returned = lax.all_to_all(
        outgoing.reshape(owners, capacity, block_size, channels),
        "wide",
        split_axis=0,
        concat_axis=0,
        tiled=True,
    )
    current = land_terms(
        count, order, asked, returned.reshape(slot_count, block_size, channels), node_blocks
    ).reshape(node_block_count * block_size, channels)
    return current


def solution(mesh):
    return jax.shard_map(
        body,
        mesh=mesh,
        in_specs=(
            P(("wide", "narrow"), None),
            P(("wide", "narrow"), None, None),
            P(("wide", "narrow"), None),
            P(("wide", "narrow")),
            P("wide"),
            P(),
            P(),
        ),
        out_specs=P(("wide", "narrow"), None),
        check_vma=False,
    )
```
